512 devices in a mesh: gx: 32 (over y, x, core), gy: 16 (over z).
Axes of the slice: x: 4, y: 4, z: 16, core: 2. Of those that a mesh axis runs over, the one named last changes fastest.
Arguments:
- right_side: float32 [3, 128, 64, 128], P(None, 'gx', 'gy'), may hold values from -10 to 10
- node_mass: float32 [128, 64, 128], P('gx', 'gy'), may hold values from 0.5 to 4
- gradients: float32 [32, 16, 8, 3, 27, 128], P('gx', 'gy'), may hold values from -3 to 3
- stiffness: float32 [32, 16, 8, 128], P('gx', 'gy'), may hold values from 0.2 to 2
- valid: int32 [32, 16, 8, 128], P('gx', 'gy'), may hold values 0 or 1
- node_base: int32 [32, 16, 8, 128], P('gx', 'gy'), may hold values from 0 to 2857, as said below
Outputs:
- solution: float32 [3, 128, 64, 128], P(None, 'gx', 'gy')
- residual: float32 [3, 128, 64, 128], P(None, 'gx', 'gy')
The draws below stay inside these ranges and needn't reach their ends.
Inputs may be any that keep to these rules, and one draw needn't show every extreme that they name: node_base = (i * 6 + j) * 130 + k with 0 <= i < 4, 0 <= j < 4, 0 <= k < 128.
All inputs are finite; a program needn't handle non-finite values. No bound on the sum of `valid` on one device may be relied on, other than what follows from the above.
Results may differ from the reference program's by a relative error of at most 0.00011.
Values sent between devices are 32-bit elements; how exact they have to be, the bound alone decides.
A program may use at most 64 MiB of HBM per device.

```python
import math
import jax
import jax.numpy as jnp
from jax import lax

CX = 4
CY = 4
NZ = 128
BLK_DEV = 8
PB = 128
TILE = 27
ITERS = 2
SWEEPS = 4
NX = 128
NY = 64
N_GX = 32
N_GY = 16


def draw_right_side(key, part):
    x_pos = jnp.arange(NX, dtype=jnp.float32).reshape(1, NX, 1, 1)
    x_ramp = 1.0 + 2.0 * x_pos / max(NX - 1, 1)
    noise_part = jnp.clip(jax.random.normal(key, (3, NX, NY, NZ), jnp.float32), -3.3, 3.3)
    values = noise_part * x_ramp
    return values.astype(jnp.float32)


def draw_node_base(key, part):
    key_list = jax.random.split(key, 4)
    dims_all = (N_GX, N_GY, BLK_DEV, PB)
    row_x = jax.random.randint(key_list[0], dims_all, 0, CX)
    row_y = jax.random.randint(key_list[1], dims_all, 0, CY)
    row_z = jax.random.randint(key_list[2], dims_all, 0, NZ)
    flattened = (row_x * (CY + 2) + row_y) * (NZ + 2) + row_z
    corner_max = ((CX - 1) * (CY + 2) + CY - 1) * (NZ + 2) + NZ - 1
    chosen = jax.random.randint(key_list[3], (), 0, PB)
    flattened = flattened.at[0, 0, 0, chosen].set(corner_max)
    flattened = flattened.at[0, 0, 0, (chosen + 1) % PB].set(0)
    return flattened.astype(jnp.int32)


def set_ends(drawn, rng, least, largest):
    place = [jax.random.randint(jax.random.fold_in(rng, axis), (), 0, length) for axis, length in enumerate(drawn.shape)]
    main_axis = drawn.shape.index(max(drawn.shape))
    neighbour = place[:main_axis] + [(place[main_axis] + 1) % drawn.shape[main_axis]] + place[main_axis + 1:]
    return drawn.at[tuple(place)].set(least).at[tuple(neighbour)].set(largest)


def level_of(own_key, extent, cuts, smallest, largest):
    factor_of = 1.0
    for axis_at, parts in cuts:
        draws = jax.random.uniform(jax.random.fold_in(jax.random.fold_in(own_key, 6), axis_at), (parts,), jnp.float32, smallest / len(cuts), largest / len(cuts))
        factor_of = factor_of * jnp.repeat(jnp.exp(draws), extent[axis_at] // parts).reshape((-1,) + (1,) * (len(extent) - 1 - axis_at))
    return factor_of


def gaussian(stream_key, shape, spread, limit, cuts=(), kind=jnp.bfloat16):
    gain = level_of(stream_key, shape, cuts, -0.22, 0.18) if cuts else 1.0
    entries = jax.random.normal(stream_key, shape, jnp.float32) * spread * gain
    return jnp.minimum(jnp.maximum(entries, -limit), limit).astype(kind)


def setup_inputs(seed: int = 0) -> dict:
    key_of = jax.random.split(jax.random.key(seed), 7)
    return {
        "right_side": draw_right_side(jax.random.fold_in(key_of[6], 71), 0),
        "node_mass": jnp.clip(jnp.exp(math.log(4.0) - 2.0794415 * jax.random.uniform(key_of[1], (NX, NY, NZ), jnp.float32) ** level_of(key_of[1], (NX, NY, NZ), ((0, 32), (1, 16)), -0.2, 0.2)), 0.5, 4.0),
        "gradients": gaussian(key_of[2], (N_GX, N_GY, BLK_DEV, 3, TILE, PB), 0.5, 3.0, ((0, 32), (1, 16)), jnp.float32),
        "stiffness": jnp.clip(jnp.exp(math.log(2.0) - 2.3025851 * jax.random.uniform(key_of[3], (N_GX, N_GY, BLK_DEV, PB), jnp.float32) ** level_of(key_of[3], (N_GX, N_GY, BLK_DEV, PB), ((0, 32), (1, 16)), -0.2, 0.2)), 0.2, 2.0),
        "valid": set_ends((jax.random.randint(key_of[4], (N_GX, N_GY, BLK_DEV, PB), 0, 8) < 7).astype(jnp.int32), jax.random.fold_in(key_of[4], 1), 0, 1),
        "node_base": draw_node_base(jax.random.fold_in(key_of[6], 71), 0),
    }


POISSON = 0.3
DAMPING = 0.7
LAPLACE_WEIGHT = 1.0


def tile_offsets(row_len, plane_len):
    corner = jnp.arange(27, dtype=jnp.int32)
    return ((corner // 9) * row_len + (corner // 3) % 3) * plane_len + corner % 3


def particle_forces(values, gradients, stiffness):
    grad_disp = jnp.einsum('...inp,...jnp->...ijp', values, gradients, precision=lax.Precision.HIGHEST)
    strain_trace = grad_disp[..., 0, 0, :] + grad_disp[..., 1, 1, :] + grad_disp[..., 2, 2, :]
    first_lame = stiffness * (POISSON / ((1.0 + POISSON) * (1.0 - 2.0 * POISSON)))
    shear_mod = stiffness * (0.5 / (1.0 + POISSON))
    identity = jnp.eye(3, dtype=values.dtype).reshape(3, 3, 1)
    stress = shear_mod[..., None, None, :] * (grad_disp + jnp.swapaxes(grad_disp, -3, -2))
    stress = stress + identity * (first_lame * strain_trace)[..., None, None, :]
    return jnp.einsum('...ijp,...jnp->...inp', stress, gradients, precision=lax.Precision.HIGHEST)


def grid_from_padded(padded, mass_diag, coupling):
    center = padded[:, 1:-1, 1:-1, 1:-1]
    beside = padded[:, 2:, 1:-1, 1:-1] + padded[:, :-2, 1:-1, 1:-1]
    beside = beside + padded[:, 1:-1, 2:, 1:-1] + padded[:, 1:-1, :-2, 1:-1]
    beside = beside + padded[:, 1:-1, 1:-1, 2:] + padded[:, 1:-1, 1:-1, :-2]
    return mass_diag * center + coupling * (6.0 * center - beside)


def grid_whole(nodal, mass_diag, coupling):
    return grid_from_padded(jnp.pad(nodal, ((0, 0), (1, 1), (1, 1), (1, 1))), mass_diag, coupling)


def aggregate(nodal):
    dims_in = nodal.shape
    leading = dims_in[:-3]
    blocked = nodal.reshape(leading + (dims_in[-3] // 2, 2, dims_in[-2] // 2, 2, dims_in[-1] // 2, 2))
    return blocked.sum(axis=(-5, -3, -1))


def expand(nodal):
    return jnp.repeat(jnp.repeat(jnp.repeat(nodal, 2, axis=-3), 2, axis=-2), 2, axis=-1)


def vcycle(source, masses, depth_index):
    mass_diag = masses[depth_index]
    coupling = LAPLACE_WEIGHT * 2.0 ** depth_index
    diagonal = mass_diag + 6.0 * coupling
    estimate = DAMPING * source / diagonal
    if depth_index == len(masses) - 1:
        for sweep_index in range(SWEEPS - 1):
            estimate = estimate + DAMPING * (source - grid_whole(estimate, mass_diag, coupling)) / diagonal
        return estimate
    remainder = source - grid_whole(estimate, mass_diag, coupling)
    estimate = estimate + expand(vcycle(aggregate(remainder), masses, depth_index + 1))
    return estimate + DAMPING * (source - grid_whole(estimate, mass_diag, coupling)) / diagonal


def stiffness_apply(nodal, gradients, effective, node_base):
    span_y = NY + 2
    span_z = NZ + 2
    padded = jnp.pad(nodal, ((0, 0), (1, 1), (1, 1), (1, 1))).reshape(3, -1)
    local_z = node_base % (NZ + 2)
    quotient = node_base // (NZ + 2)
    local_y = quotient % (CY + 2)
    local_x = quotient // (CY + 2)
    brick_x = jnp.arange(N_GX, dtype=jnp.int32).reshape(N_GX, 1, 1, 1) * CX
    brick_y = jnp.arange(N_GY, dtype=jnp.int32).reshape(1, N_GY, 1, 1) * CY
    global_base = (((brick_x + local_x) * span_y + brick_y + local_y) * span_z + local_z).astype(jnp.int32)
    offsets = tile_offsets(span_y, span_z)

    def per_column(accumulated, column):
        base_col, grad_col, stiff_col = column
        tile_index = base_col[:, :, None, :] + offsets[None, None, :, None]
        values = jnp.moveaxis(padded[:, tile_index], 0, -3)
        forces = particle_forces(values, grad_col, stiff_col)
        accumulated = accumulated.at[:, tile_index].add(jnp.moveaxis(forces, -3, 0))
        return accumulated, None

    accumulated, unused = lax.scan(per_column, jnp.zeros_like(padded), (global_base, gradients, effective))
    return accumulated.reshape(3, NX + 2, NY + 2, NZ + 2)[:, 1:-1, 1:-1, 1:-1]


def reference(right_side, node_mass, gradients, stiffness, valid, node_base):
    masses = [node_mass, aggregate(node_mass), aggregate(aggregate(node_mass))]
    effective = stiffness * valid.astype(stiffness.dtype)

    def operator(nodal):
        return node_mass * nodal + stiffness_apply(nodal, gradients, effective, node_base)

    solution = jnp.zeros_like(right_side)
    residual = right_side
    precond = vcycle(residual, masses, 0)
    direction = precond
    inner_now = jnp.sum(residual * precond)
    for iteration in range(ITERS):
        applied = operator(direction)
        step_size = inner_now / jnp.sum(direction * applied)
        solution = solution + step_size * direction
        residual = residual - step_size * applied
        if iteration + 1 < ITERS:
            precond = vcycle(residual, masses, 0)
            inner_next = jnp.sum(residual * precond)
            direction = precond + (inner_next / inner_now) * direction
            inner_now = inner_next
    return solution, residual
```

```python
import jax
import jax.numpy as jnp
from jax import lax
from jax.experimental import pallas as pl
from jax.experimental.pallas import tpu as pltpu
from jax.sharding import PartitionSpec as P

MESH = pl.DeviceIdType.MESH
F32 = jnp.float32
BF16 = jnp.bfloat16
LANES = 128
POISSON = 0.3
NEAR = tuple(
    (dx, dy)
    for dx, dy in ((0, 1), (0, -1), (1, 1), (1, -1), (-1, 1), (-1, -1), (1, 0), (-1, 0))
)
FAR = tuple(
    sorted(
        (
            (dx, dy)
            for dx in range(-4, 5)
            for dy in range(-4, 5)
            if (dx, dy) != (0, 0) and max(abs(dx) - 1, 0) + max(abs(dy) - 1, 0) <= 3
        ),
        key=lambda d: -abs(d[0]) - abs(d[1]),
    )
)
ROWS = 112


def first_cut(d, diagonal):
    if d == 0:
        return (0, 4)
    wide = 2 if diagonal else 3
    return (4 - wide, 4) if d > 0 else (0, wide)


def first_place(d, diagonal):
    if d == 0:
        return (3, 7)
    wide = 2 if diagonal else 3
    return (7, 7 + wide) if d > 0 else (3 - wide, 3)


def wide_cut(d, diagonal):
    return ((0, 4), (0, 6), (2, 6))[d + 1]


def wide_place(d, diagonal):
    return ((0, 4), (2, 8), (6, 10))[d + 1]


def thin_cut(d, diagonal):
    return ((0, 1), (1, 5), (5, 6))[d + 1]


def thin_place(d, diagonal):
    return ((0, 1), (0, 4), (3, 4))[d + 1]


def box(cut, d):
    diagonal = d[0] != 0 and d[1] != 0
    (x0, x1), (y0, y1) = cut(d[0], diagonal), cut(d[1], diagonal)
    return slice(x0, x1), slice(y0, y1)


def extent(cut, d, rows):
    sx, sy = box(cut, d)
    return (sx.stop - sx.start, sy.stop - sy.start, rows, LANES)


def kernel(n_gx, n_gy, *refs):
    (b_hbm, m_hbm, g_hbm, s_hbm, v_hbm, n_hbm, x_ref, r_ref), refs = refs[:8], refs[8:]
    first_in, wide_in, thin_in = refs[:8], refs[8:16], refs[16:24]
    one_in = (refs[24:32], refs[32:40])
    (b_in, m_in, g_in, s_in, v_in, n_in), refs = refs[40:46], refs[46:]
    (
        grad, own, rhs0, rhs1, mass, inv0, e0_ref, one_own0, one_own1, one_rhs, one_inv,
        far_own0, far_own1, far_in0, far_in1, far_rhs, far_inv, far_est, z_ref, u_ref,
        z_shift, f_rows, lhs_hi, lhs_lo, hot, rows_out, part0, part1, sums, sum_own,
        sum_own2, line_in, line_in2, near_send, near_recv, far_send, far_recv,
        line_send, line_recv, local_sem,
    ) = refs

    gx, gy = lax.axis_index("gx"), lax.axis_index("gy")

    def device(dx, dy):
        return {"gx": lax.rem(gx + (dx % n_gx), n_gx), "gy": lax.rem(gy + (dy % n_gy), n_gy)}

    loads = [
        pltpu.make_async_copy(src, dst, local_sem.at[i])
        for i, (src, dst) in enumerate(
            (
                (b_hbm, b_in), (m_hbm, m_in), (g_hbm.at[0, 0], g_in),
                (s_hbm.at[0, 0], s_in), (v_hbm.at[0, 0], v_in), (n_hbm.at[0, 0], n_in),
            )
        )
    ]
    for load in loads:
        load.start()
    partners = {(dx % n_gx, dy % n_gy) for dx, dy in FAR}
    partners |= {(d, 0) for d in range(1, n_gx)} | {(0, d) for d in range(1, n_gy)}
    partners = sorted(partners)
    barrier = pltpu.get_barrier_semaphore()
    for dx, dy in partners:
        pl.semaphore_signal(barrier, inc=1, device_id=device(dx, dy), device_id_type=MESH)
    for load in (loads[0], loads[1]):
        load.wait()
    for x in range(4):
        for y in range(4):
            for m in range(3):
                own[x, y, m : m + 1, :] = b_in[m, x, y : y + 1, :]
            own[x, y, 3:4, :] = m_in[x, y : y + 1, :]
    rhs0[3:7, 3:7] = own[:, :, 0:3, :]
    mass[3:7, 3:7] = own[:, :, 3:4, :]

    pl.semaphore_wait(barrier, len(partners))

    started = []

    def send(src, dst, group, i, d):
        copy = pltpu.make_async_remote_copy(
            src_ref=src,
            dst_ref=dst,
            send_sem=near_send.at[group, i],
            recv_sem=near_recv.at[group, NEAR.index((-d[0], -d[1]))],
            device_id=device(*d),
            device_id_type=MESH,
        )
        copy.start()
        started.append(copy)

    def arrived(dst, group, i):
        pltpu.make_async_copy(dst, dst, near_recv.at[group, i]).wait()

    def other(d):
        return NEAR.index((-d[0], -d[1]))

    for i, d in enumerate(NEAR):
        sx, sy = box(lambda *a: first_cut(*a), d)
        send(own.at[sx, sy], first_in[other(d)], 0, i, d)

    lane4 = lax.broadcasted_iota(jnp.int32, (1, 1, 3, LANES), 3)

    def ones_where(cond):
        return jnp.where(cond, 1.0, 0.0).astype(F32)

    low_ok = {s: ones_where(lane4 >= s) for s in (1, 2, 4)}
    high_ok = {s: ones_where(lane4 < LANES - s) for s in (1, 2, 4)}
    odd = {s: ones_where((lane4 & s) != 0) for s in (1, 2)}
    even = {s: ones_where((lane4 & s) == 0) for s in (1, 2)}

    def turn(v, s):
        return pltpu.roll(v, s % LANES, v.ndim - 1)

    def beside_z(v, s):
        return turn(v, s) * low_ok[s] + turn(v, -s) * high_ok[s]

    def pair_z(v, s):
        return v + turn(v, s) * odd[s] + turn(v, -s) * even[s]

    def coarser(v, s):
        nx, ny = v.shape[0] // 2, v.shape[1] // 2
        w = v.reshape((nx, 2, ny, 2) + v.shape[2:])
        w = (w[:, 0] + w[:, 1])
        w = w[:, :, 0] + w[:, :, 1]
        return pair_z(w, s)

    def finer(v):
        nx, ny = v.shape[:2]
        w = jnp.broadcast_to(v[:, None, :, None], (nx, 2, ny, 2) + v.shape[2:])
        return w.reshape((2 * nx, 2 * ny) + v.shape[2:])

    lane2 = lax.broadcasted_iota(jnp.int32, (8, LANES), 1)
    sub2 = lax.broadcasted_iota(jnp.int32, (8, LANES), 0)
    pack_mask = ones_where((lane2 & 3) == sub2)[0:3]
    mass_mask = ones_where((lane2 & 3) == 3)[0:1]
    unpack_index = (lane2 & ~3) + jnp.minimum(sub2, 2)
    inside = (
        (ones_where(gx > 0), ones_where(gx < n_gx - 1)),
        (ones_where(gy > 0), ones_where(gy < n_gy - 1)),
    )

    for load in loads[2:]:
        load.wait()
    for t in range(81):
        grad[t] = g_in[:, t // 27, t % 27, :]
    node = n_in[...]
    quotient = (node * 2017) >> 18
    k_index = node - quotient * 130
    i_index = (quotient * 43) >> 8
    j_index = quotient - i_index * 6
    effective = s_in[...] * v_in[...].astype(F32)
    z_rows = lax.broadcasted_iota(jnp.int32, (LANES, LANES), 0)
    for s in range(8):
        same = jnp.broadcast_to(k_index[s : s + 1, :], (LANES, LANES)) == z_rows
        hot[:, s * LANES : (s + 1) * LANES] = ones_where(same).astype(BF16)
    shear = effective * (0.5 / (1.0 + POISSON))
    lame = effective * (POISSON / ((1.0 + POISSON) * (1.0 - 2.0 * POISSON)))

    def particles(field, part):
        v = field[...]
        z_shift[0] = turn(v, 1) * low_ok[1]
        z_shift[1] = v
        z_shift[2] = turn(v, -1) * high_ok[1]
        i_lo, i_hi = (i_index & 1) != 0, (i_index & 2) != 0
        j_lo, j_hi = (j_index & 1) != 0, (j_index & 2) != 0

        def four(v0, v1, v2, v3, lo, hi):
            return jnp.where(hi, jnp.where(lo, v3, v2), jnp.where(lo, v1, v0))

        def gather(c, disp):
            disp = list(disp)
            for m in range(3):
                picked = [
                    [
                        jnp.take_along_axis(
                            jnp.broadcast_to(z_shift[c, x, y, m : m + 1, :], (8, LANES)),
                            k_index,
                            axis=1,
                            mode="promise_in_bounds",
                        )
                        for y in range(6)
                    ]
                    for x in range(6)
                ]
                for a in range(3):
                    row = [
                        four(*(picked[a + i][y] for i in range(4)), i_lo, i_hi) for y in range(6)
                    ]
                    for b in range(3):
                        value = four(*row[b : b + 4], j_lo, j_hi)
                        for l in range(3):
                            at = grad[l * 27 + 9 * a + 3 * b + c]
                            disp[3 * m + l] = disp[3 * m + l] + value * at
            return tuple(disp)

        zero = jnp.zeros((8, LANES), F32)
        disp = lax.fori_loop(0, 3, gather, (zero,) * 9)
        trace = lame * (disp[0] + disp[4] + disp[8])
        stress = [
            shear * (disp[3 * m + l] + disp[3 * l + m]) + (trace if m == l else 0.0)
            for m in range(3)
            for l in range(3)
        ]
        energy = sum(stress[q] * disp[q] for q in range(9))

        def scatter(c, carry):
            for m in range(3):
                spread = []
                for a in range(3):
                    force = []
                    for b in range(3):
                        t = 9 * a + 3 * b + c
                        force.append(sum(stress[3 * m + l] * grad[l * 27 + t] for l in range(3)))
                    spread.append(
                        [
                            sum(
                                jnp.where(j_index == y - b, force[b], 0.0)
                                for b in range(3)
                                if 0 <= y - b <= 3
                            )
                            for y in range(6)
                        ]
                    )
                for x in range(6):
                    for y in range(6):
                        f_rows[c * ROWS + (x * 6 + y) * 3 + m] = sum(
                            jnp.where(i_index == x - a, spread[a][y], 0.0)
                            for a in range(3)
                            if 0 <= x - a <= 3
                        )
            return carry

        lax.fori_loop(0, 3, scatter, 0)
        for s in range(8):
            rows = f_rows[:, s, :]
            high = rows.astype(BF16)
            lhs_hi[:, s * LANES : (s + 1) * LANES] = high
            lhs_lo[:, s * LANES : (s + 1) * LANES] = (rows - high.astype(F32)).astype(BF16)
        contract = (((1,), (1,)), ((), ()))
        total = lax.dot_general(lhs_hi[...], hot[...], contract, preferred_element_type=F32)
        total = total + lax.dot_general(
            lhs_lo[...], hot[...], contract, preferred_element_type=F32
        )
        rows_out[...] = (
            turn(total[0:ROWS], -1) * high_ok[1][0, 0, 0:1]
            + total[ROWS : 2 * ROWS]
            + turn(total[2 * ROWS : 3 * ROWS], 1) * low_ok[1][0, 0, 0:1]
        )
        for n in range(36):
            part[n // 6, n % 6] = rows_out[3 * n : 3 * n + 3, :]
        part[1:5, 1:5] = part[1:5, 1:5] + mass[3:7, 3:7] * field[1:5, 1:5]
        return energy

    def multigrid(turn_no, rhs, field):
        one_own = (one_own0, one_own1)[turn_no]
        far_own = (far_own0, far_own1)[turn_no]
        far_slots = (far_in0, far_in1)[turn_no]
        e0_ref[...] = inv0[...] * rhs[...]
        r0 = (
            0.3 * rhs[1:9, 1:9]
            + e0_ref[0:8, 1:9]
            + e0_ref[2:10, 1:9]
            + e0_ref[1:9, 0:8]
            + e0_ref[1:9, 2:10]
            + beside_z(e0_ref[1:9, 1:9], 1)
        )
        b1 = coarser(r0, 1)
        one_own[:, :, 0:3, :] = b1[1:3, 1:3]
        if turn_no == 0:
            mass1 = coarser(jnp.broadcast_to(mass[1:9, 1:9], (8, 8, 3, LANES)), 1)
            inv1 = 0.7 / (mass1 + 12.0)
            one_own[:, :, 3:4, :] = mass1[1:3, 1:3, 0:1]
            one_inv[1:5, 1:5] = inv1
            one_inv[1:2, 1:5] = one_inv[1:2, 1:5] * inside[0][0]
            one_inv[4:5, 1:5] = one_inv[4:5, 1:5] * inside[0][1]
            one_inv[1:5, 1:2] = one_inv[1:5, 1:2] * inside[1][0]
            one_inv[1:5, 4:5] = one_inv[1:5, 4:5] * inside[1][1]
        else:
            one_own[:, :, 3:4, :] = one_own0[:, :, 3:4, :]
        for i, d in enumerate(NEAR):
            send(one_own, one_in[turn_no][other(d)], 1 + turn_no, i, d)
        e1 = one_inv[1:5, 1:5] * b1
        r1 = 0.3 * b1[1:3, 1:3] + 2.0 * (
            e1[0:2, 1:3] + e1[2:4, 1:3] + e1[1:3, 0:2] + e1[1:3, 2:4] + beside_z(e1[1:3, 1:3], 2)
        )
        b2 = coarser(r1, 2)[0, 0]
        packed = jnp.sum(b2 * pack_mask, axis=0, keepdims=True)
        if turn_no == 0:
            mass2 = coarser(mass1[1:3, 1:3], 2)[0, 0]
            packed = packed + mass2[0:1] * mass_mask
        far_own[...] = packed
        for dx, dy in FAR:
            copy = pltpu.make_async_remote_copy(
                src_ref=far_own,
                dst_ref=far_slots.at[(4 - dx) * 9 + 4 - dy],
                send_sem=far_send.at[turn_no],
                recv_sem=far_recv.at[turn_no],
                device_id=device(dx, dy),
                device_id_type=MESH,
            )
            copy.start()
        one_rhs[2:4, 2:4] = one_own[:, :, 0:3, :]
        for i, d in enumerate(NEAR):
            got = one_in[turn_no][i]
            arrived(got, 1 + turn_no, i)
            sx, sy = slice(2 + 2 * d[0], 4 + 2 * d[0]), slice(2 + 2 * d[1], 4 + 2 * d[1])
            one_rhs[sx, sy] = got[:, :, 0:3, :]
            if turn_no == 0:
                keep = jnp.float32(1.0)
                if d[0]:
                    keep = keep * inside[0][(d[0] + 1) // 2]
                if d[1]:
                    keep = keep * inside[1][(d[1] + 1) // 2]
                beside = jnp.broadcast_to(got[:, :, 3:4, :], (2, 2, 3, LANES))
                one_inv[sx, sy] = (0.7 / (beside + 12.0)) * keep
        far_all = far_slots.at[pl.ds(0, len(FAR))]
        pltpu.make_async_copy(far_all, far_all, far_recv.at[turn_no]).wait()
        for dx, dy in FAR:
            far_rhs[dx + 4, dy + 4 : dy + 5, :] = far_slots[(dx + 4) * 9 + dy + 4]
        far_rhs[4, 4:5, :] = far_own[...]
        b = far_rhs[...]
        if turn_no == 0:
            quarter = lax.broadcasted_iota(jnp.int32, b.shape, 2) & 3
            diagonal = jnp.where(
                quarter == 0, turn(b, -3), jnp.where(quarter == 1, turn(b, -2), turn(b, -1))
            )
            at_x = lax.broadcasted_iota(jnp.int32, b.shape, 0) + (gx - 4)
            at_y = lax.broadcasted_iota(jnp.int32, b.shape, 1) + (gy - 4)
            within = (at_x >= 0) & (at_x < n_gx) & (at_y >= 0) & (at_y < n_gy)
            far_inv[...] = jnp.where(within, 0.7 / (diagonal + 24.0), 0.0)
        est = far_inv[...] * b
        for sweep in range(3):
            lo, hi = sweep + 1, 8 - sweep
            mid = est[1:-1]
            near = est[:-2] + est[2:] + pltpu.roll(mid, 1, 1) + pltpu.roll(mid, 15, 1)
            near = near + turn(mid, 4) * low_ok[4][0, :, 0:1] + turn(mid, -4) * high_ok[4][0, :, 0:1]
            est = 0.3 * mid + far_inv[lo:hi] * (b[lo:hi] + 4.0 * near)
        far_est[...] = est
        b1 = one_rhs[...]
        inv1 = one_inv[...]
        e2 = jnp.stack(
            [
                jnp.stack(
                    [
                        jnp.take_along_axis(
                            jnp.broadcast_to(far_est[x, 3 + y : 4 + y, :], (8, LANES)),
                            unpack_index,
                            axis=1,
                            mode="promise_in_bounds",
                        )[0:3]
                        for y in range(3)
                    ]
                )
                for x in range(3)
            ]
        )
        e1 = inv1 * b1 + finer(e2)
        mid = e1[1:5, 1:5]
        near = e1[0:4, 1:5] + e1[2:6, 1:5] + e1[1:5, 0:4] + e1[1:5, 2:6] + beside_z(mid, 2)
        e1 = 0.3 * mid + inv1[1:5, 1:5] * (b1[1:5, 1:5] + 2.0 * near)
        e0 = e0_ref[1:9, 1:9] + finer(e1)
        mid = e0[1:7, 1:7]
        near = e0[0:6, 1:7] + e0[2:8, 1:7] + e0[1:7, 0:6] + e0[1:7, 2:8] + beside_z(mid, 1)
        field[...] = 0.3 * mid + inv0[2:8, 2:8] * (rhs[2:8, 2:8] + near)

    for i, d in enumerate(NEAR):
        got = first_in[i]
        arrived(got, 0, i)
        sx, sy = box(first_place, d)
        rhs0[sx, sy] = got[:, :, 0:3, :]
        mass[sx, sy] = got[:, :, 3:4, :]
    inv0[...] = 0.7 / (jnp.broadcast_to(mass[...], inv0.shape) + 6.0)
    inv0[0:3] = inv0[0:3] * inside[0][0]
    inv0[7:10] = inv0[7:10] * inside[0][1]
    inv0[:, 0:3] = inv0[:, 0:3] * inside[1][0]
    inv0[:, 7:10] = inv0[:, 7:10] * inside[1][1]
    multigrid(0, rhs0, z_ref)
    particles(z_ref, part0)
    for i, d in enumerate(NEAR):
        sx, sy = box(wide_cut, d)
        send(part0.at[sx, sy], wide_in[other(d)], 3, i, d)

    def kept(d):
        keep = jnp.bool_(True)
        if d[0]:
            keep = keep & ((gx > 0) if d[0] < 0 else (gx < n_gx - 1))
        if d[1]:
            keep = keep & ((gy > 0) if d[1] < 0 else (gy < n_gy - 1))
        return jnp.where(keep, 1.0, 0.0).astype(F32)

    rhs1[...] = jnp.zeros_like(rhs1)
    rhs1[2:8, 2:8] = part0[...]
    for i, d in enumerate(NEAR):
        got = wide_in[i]
        arrived(got, 3, i)
        sx, sy = box(wide_place, d)
        rhs1[sx, sy] = rhs1[sx, sy] + got[...] * kept(d)
    multigrid(1, rhs1, u_ref)
    energy = particles(u_ref, part1)
    for i, d in enumerate(NEAR):
        sx, sy = box(thin_cut, d)
        send(part1.at[sx, sy], thin_in[other(d)], 4, i, d)

    b = rhs0[3:7, 3:7]
    w = rhs1[3:7, 3:7]
    z = z_ref[1:5, 1:5]
    u = u_ref[1:5, 1:5]
    own_mass = jnp.broadcast_to(mass[3:7, 3:7], z.shape)

    def down(v):
        return jnp.sum(v.sum(axis=(0, 1)), axis=0, keepdims=True)

    sums[...] = jnp.zeros_like(sums)
    sums[0:1] = down(b * z)
    sums[1:2] = down(z * w)
    sums[2:3] = down(b * u)
    sums[3:4] = down(w * u)
    sums[4:5] = down(own_mass * u * u) + jnp.sum(energy, axis=0, keepdims=True)
    across = jnp.broadcast_to(jnp.sum(sums[...], axis=1, keepdims=True), (8, LANES))
    sum_own[...] = jnp.sum(jnp.where(lane2 == sub2, across, 0.0), axis=0, keepdims=True)

    def along(src, slots, stage, count, step):
        for d in range(1, count):
            copy = pltpu.make_async_remote_copy(
                src_ref=src,
                dst_ref=slots.at[d - 1],
                send_sem=line_send.at[stage],
                recv_sem=line_recv.at[stage],
                device_id=device(*step(d)),
                device_id_type=MESH,
            )
            copy.start()
        whole = slots.at[pl.ds(0, count - 1)]
        pltpu.make_async_copy(whole, whole, line_recv.at[stage]).wait()
        total = src[...]
        for d in range(1, count):
            total = total + slots[d - 1]
        return total

    sum_own2[...] = along(sum_own, line_in, 0, n_gx, lambda d: (d, 0))
    total = along(sum_own2, line_in2, 1, n_gy, lambda d: (0, d))

    def scalar(i):
        index = jnp.full((8, LANES), i, jnp.int32)
        return jnp.take_along_axis(
            jnp.broadcast_to(total, (8, LANES)), index, axis=1, mode="promise_in_bounds"
        )

    bz, zw, bu, wu, uv = (scalar(i) for i in range(5))
    step0 = bz / zw
    rz1 = bz - step0 * (bu + zw) + step0 * step0 * wu
    ratio = rz1 / bz
    mixed = zw - step0 * wu
    curve = zw - 2.0 * step0 * wu + step0 * step0 * uv + 2.0 * ratio * mixed + ratio * ratio * zw
    step1 = rz1 / curve
    first = (step0 + step1 + step1 * ratio)[0:3]
    second = (step1 * step0)[0:3]

    x_ref[...] = first * z - second * u
    r_ref[...] = part1[1:5, 1:5]
    for i, d in enumerate(NEAR):
        got = thin_in[i]
        arrived(got, 4, i)
        sx, sy = box(thin_place, d)
        r_ref[sx, sy] = r_ref[sx, sy] + got[...] * kept(d)
    r_ref[...] = b - first * w + second * r_ref[...]

    for copy in started:
        copy.wait_send()
    for turn_no, slots in enumerate((far_in0, far_in1)):
        whole = slots.at[pl.ds(0, len(FAR))]
        pltpu.make_async_copy(whole, whole, far_send.at[turn_no]).wait()
    for stage, (slots, count) in enumerate(((line_in, n_gx), (line_in2, n_gy))):
        whole = slots.at[pl.ds(0, count - 1)]
        pltpu.make_async_copy(whole, whole, line_send.at[stage]).wait()


def solution(mesh):
    n_gx, n_gy = mesh.shape["gx"], mesh.shape["gy"]

    def vmem(*shape, dtype=F32):
        return pltpu.VMEM(shape, dtype)

    scratch = [vmem(*extent(first_cut, (-d[0], -d[1]), 4)) for d in NEAR]
    scratch += [vmem(*extent(wide_cut, (-d[0], -d[1]), 3)) for d in NEAR]
    scratch += [vmem(*extent(thin_cut, (-d[0], -d[1]), 3)) for d in NEAR]
    scratch += [vmem(2, 2, 4, LANES) for _ in range(16)]
    scratch += [
        vmem(3, 4, 4, LANES), vmem(4, 4, LANES), vmem(8, 3, 27, LANES),
        vmem(8, LANES), vmem(8, LANES, dtype=jnp.int32), vmem(8, LANES, dtype=jnp.int32),
    ]
    scratch += [
        vmem(81, 8, LANES),
        vmem(4, 4, 4, LANES),
        vmem(10, 10, 3, LANES),
        vmem(10, 10, 3, LANES),
        vmem(10, 10, 1, LANES),
        vmem(10, 10, 3, LANES),
        vmem(10, 10, 3, LANES),
        vmem(2, 2, 4, LANES),
        vmem(2, 2, 4, LANES),
        vmem(6, 6, 3, LANES),
        vmem(6, 6, 3, LANES),
        vmem(1, LANES),
        vmem(1, LANES),
        vmem(81, 1, LANES),
        vmem(81, 1, LANES),
        vmem(9, 16, LANES),
        vmem(9, 16, LANES),
        vmem(3, 16, LANES),
        vmem(6, 6, 3, LANES),
        vmem(6, 6, 3, LANES),
        vmem(3, 6, 6, 3, LANES),
        vmem(3 * ROWS, 8, LANES),
        vmem(3 * ROWS, 8 * LANES, dtype=BF16),
        vmem(3 * ROWS, 8 * LANES, dtype=BF16),
        vmem(LANES, 8 * LANES, dtype=BF16),
        vmem(ROWS, LANES),
        vmem(6, 6, 3, LANES),
        vmem(6, 6, 3, LANES),
        vmem(8, LANES),
        vmem(1, LANES),
        vmem(1, LANES),
        vmem(n_gx, 1, LANES),
        vmem(n_gy, 1, LANES),
        pltpu.SemaphoreType.DMA((5, 8)),
        pltpu.SemaphoreType.DMA((5, 8)),
        pltpu.SemaphoreType.DMA((2,)),
        pltpu.SemaphoreType.DMA((2,)),
        pltpu.SemaphoreType.DMA((2,)),
        pltpu.SemaphoreType.DMA((2,)),
        pltpu.SemaphoreType.DMA((6,)),
    ]

    def body(*args):
        call = pl.pallas_call(
            lambda *refs: kernel(n_gx, n_gy, *refs),
            out_shape=[jax.ShapeDtypeStruct((4, 4, 3, LANES), F32)] * 2,
            in_specs=[pl.BlockSpec(memory_space=pl.ANY)] * 6,
            out_specs=[pl.BlockSpec(memory_space=pltpu.VMEM)] * 2,
            scratch_shapes=scratch,
            compiler_params=pltpu.CompilerParams(collective_id=0, has_side_effects=True),
            name="cg",
        )
        return tuple(jnp.transpose(v, (2, 0, 1, 3)) for v in call(*args))

    field = P(None, "gx", "gy", None)
    block = P("gx", "gy", None, None)
    return jax.shard_map(
        body,
        mesh=mesh,
        in_specs=(field, P("gx", "gy", None), P("gx", "gy", None, None, None, None)) + (block,) * 3,
        out_specs=(field, field),
        check_vma=False,
    )
```

```python
import jax
import jax.numpy as jnp
from jax import lax
from jax.experimental import pallas as pl
from jax.experimental.pallas import tpu as pltpu
from jax.sharding import PartitionSpec as P

MESH = pl.DeviceIdType.MESH
F32 = jnp.float32
BF16 = jnp.bfloat16
LANES = 128
POISSON = 0.3
NEAR = tuple(
    (dx, dy)
    for dx, dy in ((0, 1), (0, -1), (1, 1), (1, -1), (-1, 1), (-1, -1), (1, 0), (-1, 0))
)
FAR = tuple(
    sorted(
        (
            (dx, dy)
            for dx in range(-4, 5)
            for dy in range(-4, 5)
            if (dx, dy) != (0, 0) and max(abs(dx) - 1, 0) + max(abs(dy) - 1, 0) <= 3
        ),
        key=lambda d: -abs(d[0]) - abs(d[1]),
    )
)
GREETED = tuple(
    (dx, dy)
    for dx in range(-3, 4)
    for dy in range(-3, 4)
    if 0 < abs(dx) + abs(dy) <= 3
) + tuple((d, 0) for d in (14, 15, 16, -15, -14))
CORNER = tuple((p, q) for p in range(4) for q in range(4) if p + q <= 3)
ROWS = 112


def first_cut(d, diagonal):
    if d == 0:
        return (0, 4)
    wide = 2 if diagonal else 3
    return (4 - wide, 4) if d > 0 else (0, wide)


def first_place(d, diagonal):
    if d == 0:
        return (3, 7)
    wide = 2 if diagonal else 3
    return (7, 7 + wide) if d > 0 else (3 - wide, 3)


def wide_cut(d, diagonal):
    return ((0, 4), (0, 6), (2, 6))[d + 1]


def wide_place(d, diagonal):
    return ((0, 4), (2, 8), (6, 10))[d + 1]


def thin_cut(d, diagonal):
    return ((0, 1), (1, 5), (5, 6))[d + 1]


def thin_place(d, diagonal):
    return ((0, 1), (0, 4), (3, 4))[d + 1]


def box(cut, d):
    diagonal = d[0] != 0 and d[1] != 0
    (x0, x1), (y0, y1) = cut(d[0], diagonal), cut(d[1], diagonal)
    return slice(x0, x1), slice(y0, y1)


def extent(cut, d, rows):
    sx, sy = box(cut, d)
    return (sx.stop - sx.start, sy.stop - sy.start, rows, LANES)


def kernel(n_gx, n_gy, *refs):
    (b_hbm, m_hbm, g_hbm, s_hbm, v_hbm, n_hbm, x_ref, r_ref), refs = refs[:8], refs[8:]
    first_in, wide_in, thin_in = refs[:8], refs[8:16], refs[16:24]
    one_in = (refs[24:32], refs[32:40])
    (b_in, m_in, s_in, v_in, n_in), refs = refs[40:45], refs[45:]
    (
        grad, own, rhs0, rhs1, mass, inv0, e0_ref, one_own0, one_own1, one_rhs, one_inv,
        far_own0, far_own1, far_in0, far_in1, far_rhs, far_inv, far_est, z_ref, u_ref,
        z_shift, f_rows, lhs_hi, lhs_lo, hot, rows_out, part0, part1, sums, sum_own,
        sum_own2, line_in, line_in2, answer, corner_out, near_send, near_recv, far_send, far_recv,
        line_send, line_recv, local_sem,
    ) = refs

    gx, gy = lax.axis_index("gx"), lax.axis_index("gy")

    def device(dx, dy):
        return {"gx": lax.rem(gx + (dx % n_gx), n_gx), "gy": lax.rem(gy + (dy % n_gy), n_gy)}

    loads = [
        pltpu.make_async_copy(src, dst, local_sem.at[i])
        for i, (src, dst) in enumerate(
            (
                (b_hbm, b_in), (m_hbm, m_in), (g_hbm, grad),
                (s_hbm.at[0, 0], s_in), (v_hbm.at[0, 0], v_in), (n_hbm.at[0, 0], n_in),
            )
        )
    ]
    for load in loads:
        load.start()
    partners = sorted({(dx % n_gx, dy % n_gy) for dx, dy in GREETED})
    barrier = pltpu.get_barrier_semaphore()
    for dx, dy in partners:
        pl.semaphore_signal(barrier, inc=1, device_id=device(dx, dy), device_id_type=MESH)
    for load in (loads[0], loads[1]):
        load.wait()
    for x in range(4):
        for y in range(4):
            for m in range(3):
                own[x, y, m : m + 1, :] = b_in[m, x, y : y + 1, :]
            own[x, y, 3:4, :] = m_in[x, y : y + 1, :]
    rhs0[3:7, 3:7] = own[:, :, 0:3, :]
    mass[3:7, 3:7] = own[:, :, 3:4, :]

    pl.semaphore_wait(barrier, len(partners))

    started = []
    closers = []

    def close():
        for copy in started:
            copy.wait_send()
        for whole, sem in closers:
            pltpu.make_async_copy(whole, whole, sem).wait()

    def send(src, dst, group, i, d):
        copy = pltpu.make_async_remote_copy(
            src_ref=src,
            dst_ref=dst,
            send_sem=near_send.at[group, i],
            recv_sem=near_recv.at[group, NEAR.index((-d[0], -d[1]))],
            device_id=device(*d),
            device_id_type=MESH,
        )
        copy.start()
        started.append(copy)

    def arrived(dst, group, i):
        pltpu.make_async_copy(dst, dst, near_recv.at[group, i]).wait()

    def other(d):
        return NEAR.index((-d[0], -d[1]))

    for i, d in enumerate(NEAR):
        sx, sy = box(first_cut, d)
        send(own.at[sx, sy], first_in[other(d)], 0, i, d)

    lane4 = lax.broadcasted_iota(jnp.int32, (1, 1, 3, LANES), 3)

    def ones_where(cond):
        return jnp.where(cond, 1.0, 0.0).astype(F32)

    low_ok = {s: ones_where(lane4 >= s) for s in (1, 2, 4)}
    high_ok = {s: ones_where(lane4 < LANES - s) for s in (1, 2, 4)}
    odd = {s: ones_where((lane4 & s) != 0) for s in (1, 2)}
    even = {s: ones_where((lane4 & s) == 0) for s in (1, 2)}

    def turn(v, s):
        return pltpu.roll(v, s % LANES, v.ndim - 1)

    def beside_z(v, s):
        return turn(v, s) * low_ok[s] + turn(v, -s) * high_ok[s]

    def pair_z(v, s):
        return v + turn(v, s) * odd[s] + turn(v, -s) * even[s]

    def coarser(v, s):
        nx, ny = v.shape[0] // 2, v.shape[1] // 2
        w = v.reshape((nx, 2, ny, 2) + v.shape[2:])
        w = (w[:, 0] + w[:, 1])
        w = w[:, :, 0] + w[:, :, 1]
        return pair_z(w, s)

    def finer(v):
        nx, ny = v.shape[:2]
        w = jnp.broadcast_to(v[:, None, :, None], (nx, 2, ny, 2) + v.shape[2:])
        return w.reshape((2 * nx, 2 * ny) + v.shape[2:])

    lane2 = lax.broadcasted_iota(jnp.int32, (8, LANES), 1)
    sub2 = lax.broadcasted_iota(jnp.int32, (8, LANES), 0)
    pack_mask = ones_where((lane2 & 3) == sub2)[0:3]
    mass_mask = ones_where((lane2 & 3) == 3)[0:1]
    unpack_index = (lane2 & ~3) + jnp.minimum(sub2, 2)
    inside = (
        (ones_where(gx > 0), ones_where(gx < n_gx - 1)),
        (ones_where(gy > 0), ones_where(gy < n_gy - 1)),
    )

    for load in loads[2:]:
        load.wait()
    node = n_in[...]
    quotient = (node * 2017) >> 18
    k_index = node - quotient * 130
    i_index = (quotient * 43) >> 8
    j_index = quotient - i_index * 6
    effective = s_in[...] * v_in[...].astype(F32)
    z_rows = lax.broadcasted_iota(jnp.int32, (LANES, LANES), 0)
    for s in range(8):
        same = jnp.broadcast_to(k_index[s : s + 1, :], (LANES, LANES)) == z_rows
        hot[:, s * LANES : (s + 1) * LANES] = ones_where(same).astype(BF16)
    shear = effective * (0.5 / (1.0 + POISSON))
    lame = effective * (POISSON / ((1.0 + POISSON) * (1.0 - 2.0 * POISSON)))

    def strains(field):
        v = field[...]
        z_shift[0] = turn(v, 1) * low_ok[1]
        z_shift[1] = v
        z_shift[2] = turn(v, -1) * high_ok[1]
        i_lo, i_hi = (i_index & 1) != 0, (i_index & 2) != 0
        j_lo, j_hi = (j_index & 1) != 0, (j_index & 2) != 0

        def four(v0, v1, v2, v3, lo, hi):
            return jnp.where(hi, jnp.where(lo, v3, v2), jnp.where(lo, v1, v0))

        def gather(c, disp):
            disp = list(disp)
            for m in range(3):
                picked = [
                    [
                        jnp.take_along_axis(
                            jnp.broadcast_to(z_shift[c, x, y, m : m + 1, :], (8, LANES)),
                            k_index,
                            axis=1,
                            mode="promise_in_bounds",
                        )
                        for y in range(6)
                    ]
                    for x in range(6)
                ]
                for a in range(3):
                    row = [
                        four(*(picked[a + i][y] for i in range(4)), i_lo, i_hi) for y in range(6)
                    ]
                    for b in range(3):
                        value = four(*row[b : b + 4], j_lo, j_hi)
                        for l in range(3):
                            at = grad[l * 27 + 9 * a + 3 * b + c]
                            disp[3 * m + l] = disp[3 * m + l] + value * at
            return tuple(disp)

        zero = jnp.zeros((8, LANES), F32)
        disp = lax.fori_loop(0, 3, gather, (zero,) * 9)
        trace = lame * (disp[0] + disp[4] + disp[8])
        stress = [
            shear * (disp[3 * m + l] + disp[3 * l + m]) + (trace if m == l else 0.0)
            for m in range(3)
            for l in range(3)
        ]
        return stress, sum(stress[q] * disp[q] for q in range(9))

    def forces(stress, field, part):
        def scatter(c, carry):
            for m in range(3):
                spread = []
                for a in range(3):
                    force = []
                    for b in range(3):
                        t = 9 * a + 3 * b + c
                        force.append(sum(stress[3 * m + l] * grad[l * 27 + t] for l in range(3)))
                    spread.append(
                        [
                            sum(
                                jnp.where(j_index == y - b, force[b], 0.0)
                                for b in range(3)
                                if 0 <= y - b <= 3
                            )
                            for y in range(6)
                        ]
                    )
                for x in range(6):
                    for y in range(6):
                        row = pl.multiple_of((c * ROWS + (x * 6 + y) * 3 + m) * 8, 8)
                        f_rows[pl.ds(row, 8), :] = sum(
                            jnp.where(i_index == x - a, spread[a][y], 0.0)
                            for a in range(3)
                            if 0 <= x - a <= 3
                        )
            return carry

        lax.fori_loop(0, 3, scatter, 0)
        for s in range(8):
            rows = f_rows[pl.ds(s, 3 * ROWS, stride=8), :]
            high = rows.astype(BF16)
            lhs_hi[:, s * LANES : (s + 1) * LANES] = high
            lhs_lo[:, s * LANES : (s + 1) * LANES] = (rows - high.astype(F32)).astype(BF16)
        contract = (((1,), (1,)), ((), ()))
        total = lax.dot_general(lhs_hi[...], hot[...], contract, preferred_element_type=F32)
        total = total + lax.dot_general(
            lhs_lo[...], hot[...], contract, preferred_element_type=F32
        )
        rows_out[...] = (
            turn(total[0:ROWS], -1) * high_ok[1][0, 0, 0:1]
            + total[ROWS : 2 * ROWS]
            + turn(total[2 * ROWS : 3 * ROWS], 1) * low_ok[1][0, 0, 0:1]
        )
        for n in range(36):
            part[n // 6, n % 6] = rows_out[3 * n : 3 * n + 3, :]
        part[1:5, 1:5] = part[1:5, 1:5] + mass[3:7, 3:7] * field[1:5, 1:5]

    def multigrid(turn_no, rhs, field, meanwhile):
        one_own = (one_own0, one_own1)[turn_no]
        far_own = (far_own0, far_own1)[turn_no]
        far_slots = (far_in0, far_in1)[turn_no]
        e0_ref[...] = inv0[...] * rhs[...]
        r0 = (
            0.3 * rhs[1:9, 1:9]
            + e0_ref[0:8, 1:9]
            + e0_ref[2:10, 1:9]
            + e0_ref[1:9, 0:8]
            + e0_ref[1:9, 2:10]
            + beside_z(e0_ref[1:9, 1:9], 1)
        )
        b1 = coarser(r0, 1)
        one_own[:, :, 0:3, :] = b1[1:3, 1:3]
        if turn_no == 0:
            mass1 = coarser(jnp.broadcast_to(mass[1:9, 1:9], (8, 8, 3, LANES)), 1)
            inv1 = 0.7 / (mass1 + 12.0)
            one_own[:, :, 3:4, :] = mass1[1:3, 1:3, 0:1]
            one_inv[1:5, 1:5] = inv1
            one_inv[1:2, 1:5] = one_inv[1:2, 1:5] * inside[0][0]
            one_inv[4:5, 1:5] = one_inv[4:5, 1:5] * inside[0][1]
            one_inv[1:5, 1:2] = one_inv[1:5, 1:2] * inside[1][0]
            one_inv[1:5, 4:5] = one_inv[1:5, 4:5] * inside[1][1]
        else:
            one_own[:, :, 3:4, :] = one_own0[:, :, 3:4, :]
        e1 = one_inv[1:5, 1:5] * b1
        r1 = 0.3 * b1[1:3, 1:3] + 2.0 * (
            e1[0:2, 1:3] + e1[2:4, 1:3] + e1[1:3, 0:2] + e1[1:3, 2:4] + beside_z(e1[1:3, 1:3], 2)
        )
        b2 = coarser(r1, 2)[0, 0]
        packed = jnp.sum(b2 * pack_mask, axis=0, keepdims=True)
        if turn_no == 0:
            mass2 = coarser(mass1[1:3, 1:3], 2)[0, 0]
            packed = packed + mass2[0:1] * mass_mask
        far_own[...] = packed
        for dx, dy in FAR:
            copy = pltpu.make_async_remote_copy(
                src_ref=far_own,
                dst_ref=far_slots.at[(4 - dx) * 9 + 4 - dy],
                send_sem=far_send.at[turn_no],
                recv_sem=far_recv.at[turn_no],
                device_id=device(dx, dy),
                device_id_type=MESH,
            )
            copy.start()
        for i, d in enumerate(NEAR):
            send(one_own, one_in[turn_no][other(d)], 1 + turn_no, i, d)
        meanwhile()
        one_rhs[2:4, 2:4] = one_own[:, :, 0:3, :]
        for i, d in enumerate(NEAR):
            got = one_in[turn_no][i]
            arrived(got, 1 + turn_no, i)
            sx, sy = slice(2 + 2 * d[0], 4 + 2 * d[0]), slice(2 + 2 * d[1], 4 + 2 * d[1])
            one_rhs[sx, sy] = got[:, :, 0:3, :]
            if turn_no == 0:
                keep = jnp.float32(1.0)
                if d[0]:
                    keep = keep * inside[0][(d[0] + 1) // 2]
                if d[1]:
                    keep = keep * inside[1][(d[1] + 1) // 2]
                beside = jnp.broadcast_to(got[:, :, 3:4, :], (2, 2, 3, LANES))
                one_inv[sx, sy] = (0.7 / (beside + 12.0)) * keep
        far_all = far_slots.at[pl.ds(0, len(FAR))]
        closers.append((far_all, far_send.at[turn_no]))
        pltpu.make_async_copy(far_all, far_all, far_recv.at[turn_no]).wait()
        for dx, dy in FAR:
            far_rhs[dx + 4, dy + 4 : dy + 5, :] = far_slots[(dx + 4) * 9 + dy + 4]
        far_rhs[4, 4:5, :] = far_own[...]
        b = far_rhs[...]
        if turn_no == 0:
            quarter = lax.broadcasted_iota(jnp.int32, b.shape, 2) & 3
            diagonal = jnp.where(
                quarter == 0, turn(b, -3), jnp.where(quarter == 1, turn(b, -2), turn(b, -1))
            )
            at_x = lax.broadcasted_iota(jnp.int32, b.shape, 0) + (gx - 4)
            at_y = lax.broadcasted_iota(jnp.int32, b.shape, 1) + (gy - 4)
            within = (at_x >= 0) & (at_x < n_gx) & (at_y >= 0) & (at_y < n_gy)
            far_inv[...] = jnp.where(within, 0.7 / (diagonal + 24.0), 0.0)
        est = far_inv[...] * b
        for sweep in range(3):
            lo, hi = sweep + 1, 8 - sweep
            mid = est[1:-1]
            near = est[:-2] + est[2:] + pltpu.roll(mid, 1, 1) + pltpu.roll(mid, 15, 1)
            near = near + turn(mid, 4) * low_ok[4][0, :, 0:1] + turn(mid, -4) * high_ok[4][0, :, 0:1]
            est = 0.3 * mid + far_inv[lo:hi] * (b[lo:hi] + 4.0 * near)
        far_est[...] = est
        b1 = one_rhs[...]
        inv1 = one_inv[...]
        e2 = jnp.stack(
            [
                jnp.stack(
                    [
                        jnp.take_along_axis(
                            jnp.broadcast_to(far_est[x, 3 + y : 4 + y, :], (8, LANES)),
                            unpack_index,
                            axis=1,
                            mode="promise_in_bounds",
                        )[0:3]
                        for y in range(3)
                    ]
                )
                for x in range(3)
            ]
        )
        e1 = inv1 * b1 + finer(e2)
        mid = e1[1:5, 1:5]
        near = e1[0:4, 1:5] + e1[2:6, 1:5] + e1[1:5, 0:4] + e1[1:5, 2:6] + beside_z(mid, 2)
        e1 = 0.3 * mid + inv1[1:5, 1:5] * (b1[1:5, 1:5] + 2.0 * near)
        e0 = e0_ref[1:9, 1:9] + finer(e1)
        mid = e0[1:7, 1:7]
        near = e0[0:6, 1:7] + e0[2:8, 1:7] + e0[1:7, 0:6] + e0[1:7, 2:8] + beside_z(mid, 1)
        field[...] = 0.3 * mid + inv0[2:8, 2:8] * (rhs[2:8, 2:8] + near)

    def down(v):
        return jnp.sum(v.sum(axis=(0, 1)), axis=0, keepdims=True)

    def early_sums():
        sums[...] = jnp.zeros_like(sums)
        sums[0:1] = down(rhs0[3:7, 3:7] * z_ref[1:5, 1:5])
        sums[1:2] = down(rhs1[3:7, 3:7] * z_ref[1:5, 1:5])

    for i, d in enumerate(NEAR):
        got = first_in[i]
        arrived(got, 0, i)
        sx, sy = box(first_place, d)
        rhs0[sx, sy] = got[:, :, 0:3, :]
        mass[sx, sy] = got[:, :, 3:4, :]
    inv0[...] = 0.7 / (jnp.broadcast_to(mass[...], inv0.shape) + 6.0)
    inv0[0:3] = inv0[0:3] * inside[0][0]
    inv0[7:10] = inv0[7:10] * inside[0][1]
    inv0[:, 0:3] = inv0[:, 0:3] * inside[1][0]
    inv0[:, 7:10] = inv0[:, 7:10] * inside[1][1]
    multigrid(0, rhs0, z_ref, lambda: None)
    stress, _ = strains(z_ref)
    forces(stress, z_ref, part0)
    for i, d in enumerate(NEAR):
        if d[0] and d[1]:
            n = (2, 3, 4, 5).index(i)
            for k, (p, q) in enumerate(CORNER):
                corner_out[n, k] = part0[5 - p if d[0] > 0 else p, 5 - q if d[1] > 0 else q]
            send(corner_out.at[n], wide_in[other(d)], 3, i, d)
        else:
            sx, sy = box(wide_cut, d)
            send(part0.at[sx, sy], wide_in[other(d)], 3, i, d)

    def kept(d):
        keep = jnp.bool_(True)
        if d[0]:
            keep = keep & ((gx > 0) if d[0] < 0 else (gx < n_gx - 1))
        if d[1]:
            keep = keep & ((gy > 0) if d[1] < 0 else (gy < n_gy - 1))
        return jnp.where(keep, 1.0, 0.0).astype(F32)

    rhs1[...] = jnp.zeros_like(rhs1)
    rhs1[2:8, 2:8] = part0[...]
    for i, d in enumerate(NEAR):
        got = wide_in[i]
        arrived(got, 3, i)
        if d[0] and d[1]:
            for k, (p, q) in enumerate(CORNER):
                x, y = (3 - p if d[0] < 0 else 6 + p), (3 - q if d[1] < 0 else 6 + q)
                rhs1[x, y] = rhs1[x, y] + got[k] * kept(d)
        else:
            sx, sy = box(wide_place, d)
            rhs1[sx, sy] = rhs1[sx, sy] + got[...] * kept(d)
    multigrid(1, rhs1, u_ref, early_sums)
    stress, energy = strains(u_ref)

    def line_start(src, slots, stage, count, step):
        for d in range(1, count):
            copy = pltpu.make_async_remote_copy(
                src_ref=src,
                dst_ref=slots.at[d - 1],
                send_sem=line_send.at[stage],
                recv_sem=line_recv.at[stage],
                device_id=device(*step(d)),
                device_id_type=MESH,
            )
            copy.start()
        closers.append((slots.at[pl.ds(0, count - 1)], line_send.at[stage]))

    def line_end(src, slots, stage, count):
        whole = slots.at[pl.ds(0, count - 1)]
        pltpu.make_async_copy(whole, whole, line_recv.at[stage]).wait()
        total = src[...]
        for d in range(1, count):
            total = total + slots[d - 1]
        return total

    b = rhs0[3:7, 3:7]
    w = rhs1[3:7, 3:7]
    z = z_ref[1:5, 1:5]
    u = u_ref[1:5, 1:5]
    own_mass = jnp.broadcast_to(mass[3:7, 3:7], z.shape)
    sums[2:3] = down(b * u)
    sums[3:4] = down(w * u)
    sums[4:5] = down(own_mass * u * u) + jnp.sum(energy, axis=0, keepdims=True)
    across = jnp.broadcast_to(jnp.sum(sums[...], axis=1, keepdims=True), (8, LANES))
    sum_own[...] = jnp.sum(jnp.where(lane2 == sub2, across, 0.0), axis=0, keepdims=True)
    line_start(sum_own, line_in, 0, n_gx, lambda d: ((16 + d) % n_gx if d != 16 else 16, 0))
    forces(stress, u_ref, part1)
    for i, d in enumerate(NEAR):
        sx, sy = box(thin_cut, d)
        send(part1.at[sx, sy], thin_in[other(d)], 4, i, d)
    sum_own2[...] = line_end(sum_own, line_in, 0, n_gx)
    line_start(sum_own2, line_in2, 1, n_gy, lambda d: (0, (8 + d) % n_gy if d != 8 else 8))
    total = line_end(sum_own2, line_in2, 1, n_gy)

    def scalar(i):
        index = jnp.full((8, LANES), i, jnp.int32)
        return jnp.take_along_axis(
            jnp.broadcast_to(total, (8, LANES)), index, axis=1, mode="promise_in_bounds"
        )

    bz, zw, bu, wu, uv = (scalar(i) for i in range(5))
    step0 = bz / zw
    rz1 = bz - step0 * (bu + zw) + step0 * step0 * wu
    ratio = rz1 / bz
    mixed = zw - step0 * wu
    curve = zw - 2.0 * step0 * wu + step0 * step0 * uv + 2.0 * ratio * mixed + ratio * ratio * zw
    step1 = rz1 / curve
    first = (step0 + step1 + step1 * ratio)[0:3]
    second = (step1 * step0)[0:3]

    answer[...] = first * z - second * u
    for n in range(48):
        x, y, m = n // 12, n // 3 % 4, n % 3
        x_ref[m, x, y : y + 1, :] = answer[x, y, m : m + 1, :]
    e0_ref[0:4, 0:4] = part1[1:5, 1:5]
    for i, d in enumerate(NEAR):
        arrived(thin_in[i], 4, i)
        sx, sy = box(thin_place, d)
        e0_ref[sx, sy] = e0_ref[sx, sy] + thin_in[i][...] * kept(d)
    answer[...] = b - first * w + second * e0_ref[0:4, 0:4]
    for n in range(48):
        x, y, m = n // 12, n // 3 % 4, n % 3
        r_ref[m, x, y : y + 1, :] = answer[x, y, m : m + 1, :]
    close()


def solution(mesh):
    n_gx, n_gy = mesh.shape["gx"], mesh.shape["gy"]

    def vmem(*shape, dtype=F32):
        return pltpu.VMEM(shape, dtype)

    scratch = [vmem(*extent(first_cut, (-d[0], -d[1]), 4)) for d in NEAR]
    scratch += [
        vmem(10, 3, LANES) if d[0] and d[1] else vmem(*extent(wide_cut, (-d[0], -d[1]), 3))
        for d in NEAR
    ]
    scratch += [vmem(*extent(thin_cut, (-d[0], -d[1]), 3)) for d in NEAR]
    scratch += [vmem(2, 2, 4, LANES) for _ in range(16)]
    scratch += [
        vmem(3, 4, 4, LANES), vmem(4, 4, LANES),
        vmem(8, LANES), vmem(8, LANES, dtype=jnp.int32), vmem(8, LANES, dtype=jnp.int32),
    ]
    scratch += [
        vmem(81, 8, LANES),
        vmem(4, 4, 4, LANES),
        vmem(10, 10, 3, LANES),
        vmem(10, 10, 3, LANES),
        vmem(10, 10, 1, LANES),
        vmem(10, 10, 3, LANES),
        vmem(10, 10, 3, LANES),
        vmem(2, 2, 4, LANES),
        vmem(2, 2, 4, LANES),
        vmem(6, 6, 3, LANES),
        vmem(6, 6, 3, LANES),
        vmem(1, LANES),
        vmem(1, LANES),
        vmem(81, 1, LANES),
        vmem(81, 1, LANES),
        vmem(9, 16, LANES),
        vmem(9, 16, LANES),
        vmem(3, 16, LANES),
        vmem(6, 6, 3, LANES),
        vmem(6, 6, 3, LANES),
        vmem(3, 6, 6, 3, LANES),
        vmem(3 * ROWS * 8, LANES),
        vmem(3 * ROWS, 8 * LANES, dtype=BF16),
        vmem(3 * ROWS, 8 * LANES, dtype=BF16),
        vmem(LANES, 8 * LANES, dtype=BF16),
        vmem(ROWS, LANES),
        vmem(6, 6, 3, LANES),
        vmem(6, 6, 3, LANES),
        vmem(8, LANES),
        vmem(1, LANES),
        vmem(1, LANES),
        vmem(n_gx, 1, LANES),
        vmem(n_gy, 1, LANES),
        vmem(4, 4, 3, LANES),
        vmem(4, 10, 3, LANES),
        pltpu.SemaphoreType.DMA((5, 8)),
        pltpu.SemaphoreType.DMA((5, 8)),
        pltpu.SemaphoreType.DMA((2,)),
        pltpu.SemaphoreType.DMA((2,)),
        pltpu.SemaphoreType.DMA((2,)),
        pltpu.SemaphoreType.DMA((2,)),
        pltpu.SemaphoreType.DMA((6,)),
    ]

    def body(right, mass, gradients, *rest):
        by_tile = jnp.transpose(gradients[0, 0], (1, 2, 0, 3)).reshape(81, 8, LANES)
        args = (right, mass, by_tile) + rest
        call = pl.pallas_call(
            lambda *refs: kernel(n_gx, n_gy, *refs),
            out_shape=[jax.ShapeDtypeStruct((3, 4, 4, LANES), F32)] * 2,
            in_specs=[pl.BlockSpec(memory_space=pl.ANY)] * 6,
            out_specs=[pl.BlockSpec(memory_space=pltpu.VMEM)] * 2,
            scratch_shapes=scratch,
            compiler_params=pltpu.CompilerParams(collective_id=0, has_side_effects=True),
            name="cg",
        )
        return tuple(call(*args))

    field = P(None, "gx", "gy", None)
    block = P("gx", "gy", None, None)
    return jax.shard_map(
        body,
        mesh=mesh,
        in_specs=(field, P("gx", "gy", None), P("gx", "gy", None, None, None, None)) + (block,) * 3,
        out_specs=(field, field),
        check_vma=False,
    )
```

```python
import jax
import jax.numpy as jnp
from jax import lax
from jax.experimental import pallas as pl
from jax.experimental.pallas import tpu as pltpu
from jax.sharding import PartitionSpec as P

MESH = pl.DeviceIdType.MESH
F32 = jnp.float32
BF16 = jnp.bfloat16
LANES = 128
POISSON = 0.3
NEAR = tuple(
    (dx, dy)
    for dx, dy in ((0, 1), (0, -1), (1, 1), (1, -1), (-1, 1), (-1, -1), (1, 0), (-1, 0))
)
FAR = tuple(
    sorted(
        (
            (dx, dy)
            for dx in range(-4, 5)
            for dy in range(-4, 5)
            if (dx, dy) != (0, 0) and max(abs(dx) - 1, 0) + max(abs(dy) - 1, 0) <= 3
        ),
        key=lambda d: -abs(d[0]) - abs(d[1]),
    )
)
GREETED = tuple(
    (dx, dy)
    for dx in range(-3, 4)
    for dy in range(-3, 4)
    if 0 < abs(dx) + abs(dy) <= 3
) + tuple((d, 0) for d in (14, 15, 16, -15, -14))
CORNER = tuple((p, q) for p in range(3) for q in range(3) if p + q <= 3)
ROWS = 112


def first_cut(d, diagonal):
    if d == 0:
        return (0, 4)
    wide = 2 if diagonal else 3
    return (4 - wide, 4) if d > 0 else (0, wide)


def first_place(d, diagonal):
    if d == 0:
        return (3, 7)
    wide = 2 if diagonal else 3
    return (7, 7 + wide) if d > 0 else (3 - wide, 3)


def wide_cut(d, diagonal):
    return ((0, 3), (0, 6), (3, 6))[d + 1]


def wide_place(d, diagonal):
    return ((1, 4), (2, 8), (6, 9))[d + 1]


def thin_cut(d, diagonal):
    return ((0, 1), (1, 5), (5, 6))[d + 1]


def thin_place(d, diagonal):
    return ((0, 1), (0, 4), (3, 4))[d + 1]


def box(cut, d):
    diagonal = d[0] != 0 and d[1] != 0
    (x0, x1), (y0, y1) = cut(d[0], diagonal), cut(d[1], diagonal)
    return slice(x0, x1), slice(y0, y1)


def extent(cut, d, rows):
    sx, sy = box(cut, d)
    return (sx.stop - sx.start, sy.stop - sy.start, rows, LANES)


def kernel(n_gx, n_gy, *refs):
    (b_hbm, m_hbm, g_hbm, s_hbm, v_hbm, n_hbm, x_ref, r_ref), refs = refs[:8], refs[8:]
    first_in, wide_in, thin_in = refs[:8], refs[8:16], refs[16:24]
    one_in = (refs[24:32], refs[32:40])
    (b_in, m_in, s_in, v_in, n_in), refs = refs[40:45], refs[45:]
    (
        grad, own, rhs0, rhs1, mass, inv0, e0_ref, one_own0, one_own1, one_rhs, one_inv,
        far_own0, far_own1, far_in0, far_in1, far_rhs, far_inv, far_est, z_ref, u_ref,
        z_shift, f_rows, hot, rows_out, part0, part1, sums, sum_own,
        sum_own2, line_in, line_in2, answer, corner_out, few_out, few_in, one_pad, fine_pad, one_share, mass_rows, inv_rows, near_send, near_recv, far_send, far_recv,
        line_send, line_recv, local_sem,
    ) = refs

    gx, gy = lax.axis_index("gx"), lax.axis_index("gy")

    def device(dx, dy):
        return {"gx": lax.rem(gx + (dx % n_gx), n_gx), "gy": lax.rem(gy + (dy % n_gy), n_gy)}

    loads = [
        pltpu.make_async_copy(src, dst, local_sem.at[i])
        for i, (src, dst) in enumerate(
            (
                (b_hbm, b_in), (m_hbm, m_in), (g_hbm, grad),
                (s_hbm.at[0, 0], s_in), (v_hbm.at[0, 0], v_in), (n_hbm.at[0, 0], n_in),
            )
        )
    ]
    for load in loads:
        load.start()
    partners = list(NEAR) + sorted(set(GREETED) - set(NEAR))
    barrier = pltpu.get_barrier_semaphore()
    for dx, dy in partners:
        pl.semaphore_signal(barrier, inc=1, device_id=device(dx, dy), device_id_type=MESH)
    for load in (loads[0], loads[1]):
        load.wait()
    for x in range(4):
        for y in range(4):
            for m in range(3):
                own[x, y, m : m + 1, :] = b_in[m, x, y : y + 1, :]
            own[x, y, 3:4, :] = m_in[x, y : y + 1, :]
    rhs0[3:7, 3:7] = own[:, :, 0:3, :]
    mass[3:7, 3:7] = own[:, :, 3:4, :]

    pl.semaphore_wait(barrier, len(partners))

    started = []
    closers = []

    def close():
        for copy in started:
            copy.wait_send()
        for whole, sem in closers:
            pltpu.make_async_copy(whole, whole, sem).wait()

    def send(src, dst, group, i, d):
        copy = pltpu.make_async_remote_copy(
            src_ref=src,
            dst_ref=dst,
            send_sem=near_send.at[group, i],
            recv_sem=near_recv.at[group, NEAR.index((-d[0], -d[1]))],
            device_id=device(*d),
            device_id_type=MESH,
        )
        copy.start()
        started.append(copy)

    def arrived(dst, group, i):
        pltpu.make_async_copy(dst, dst, near_recv.at[group, i]).wait()

    def other(d):
        return NEAR.index((-d[0], -d[1]))

    for i, d in enumerate(NEAR):
        sx, sy = box(first_cut, d)
        send(own.at[sx, sy], first_in[other(d)], 0, i, d)

    lane4 = lax.broadcasted_iota(jnp.int32, (1, 1, 3, LANES), 3)

    def ones_where(cond):
        return jnp.where(cond, 1.0, 0.0).astype(F32)

    low_ok = {s: ones_where(lane4 >= s) for s in (1, 2, 4)}
    high_ok = {s: ones_where(lane4 < LANES - s) for s in (1, 2, 4)}
    odd = {s: ones_where((lane4 & s) != 0) for s in (1, 2)}
    even = {s: ones_where((lane4 & s) == 0) for s in (1, 2)}

    def turn(v, s):
        return pltpu.roll(v, s % LANES, v.ndim - 1)

    def beside_z(v, s):
        return turn(v, s) * low_ok[s] + turn(v, -s) * high_ok[s]

    def pair_z(v, s):
        return v + turn(v, s) * odd[s] + turn(v, -s) * even[s]

    def coarser(v, s):
        nx, ny = v.shape[0] // 2, v.shape[1] // 2
        w = v.reshape((nx, 2, ny, 2) + v.shape[2:])
        w = (w[:, 0] + w[:, 1])
        w = w[:, :, 0] + w[:, :, 1]
        return pair_z(w, s)

    def finer(v):
        nx, ny = v.shape[:2]
        w = jnp.broadcast_to(v[:, None, :, None], (nx, 2, ny, 2) + v.shape[2:])
        return w.reshape((2 * nx, 2 * ny) + v.shape[2:])

    lane2 = lax.broadcasted_iota(jnp.int32, (8, LANES), 1)
    sub2 = lax.broadcasted_iota(jnp.int32, (8, LANES), 0)
    pack_mask = ones_where((lane2 & 3) == sub2)[0:3]
    mass_mask = ones_where((lane2 & 3) == 3)[0:1]
    unpack_index = (lane2 & ~3) + jnp.minimum(sub2, 2)
    inside = (
        (ones_where(gx > 0), ones_where(gx < n_gx - 1)),
        (ones_where(gy > 0), ones_where(gy < n_gy - 1)),
    )

    for load in loads[2:]:
        load.wait()
    node = n_in[...]
    quotient = (node * 2017) >> 18
    k_index = node - quotient * 130
    i_index = (quotient * 43) >> 8
    j_index = quotient - i_index * 6
    effective = s_in[...] * v_in[...].astype(F32)
    z_rows = lax.broadcasted_iota(jnp.int32, (LANES, LANES), 0)
    for s in range(8):
        same = jnp.broadcast_to(k_index[s : s + 1, :], (LANES, LANES)) == z_rows
        hot[:, s * LANES : (s + 1) * LANES] = ones_where(same).astype(BF16)
    shear = effective * (0.5 / (1.0 + POISSON))
    lame = effective * (POISSON / ((1.0 + POISSON) * (1.0 - 2.0 * POISSON)))

    def strains(field):
        v = field[...]
        z_shift[0] = turn(v, 1) * low_ok[1]
        z_shift[1] = v
        z_shift[2] = turn(v, -1) * high_ok[1]
        i_lo, i_hi = (i_index & 1) != 0, (i_index & 2) != 0
        j_lo, j_hi = (j_index & 1) != 0, (j_index & 2) != 0

        def four(v0, v1, v2, v3, lo, hi):
            return jnp.where(hi, jnp.where(lo, v3, v2), jnp.where(lo, v1, v0))

        def gather(c, disp):
            disp = list(disp)
            for m in range(3):
                picked = [
                    [
                        jnp.take_along_axis(
                            jnp.broadcast_to(z_shift[c, x, y, m : m + 1, :], (8, LANES)),
                            k_index,
                            axis=1,
                            mode="promise_in_bounds",
                        )
                        for y in range(6)
                    ]
                    for x in range(6)
                ]
                for a in range(3):
                    row = [
                        four(*(picked[a + i][y] for i in range(4)), i_lo, i_hi) for y in range(6)
                    ]
                    for b in range(3):
                        value = four(*row[b : b + 4], j_lo, j_hi)
                        for l in range(3):
                            at = grad[l * 27 + 9 * a + 3 * b + c]
                            disp[3 * m + l] = disp[3 * m + l] + value * at
            return tuple(disp)

        zero = jnp.zeros((8, LANES), F32)
        disp = lax.fori_loop(0, 3, gather, (zero,) * 9)
        trace = lame * (disp[0] + disp[4] + disp[8])
        stress = [
            shear * (disp[3 * m + l] + disp[3 * l + m]) + (trace if m == l else 0.0)
            for m in range(3)
            for l in range(3)
        ]
        return stress, sum(stress[q] * disp[q] for q in range(9))

    def forces(stress, field, part):
        def scatter(c, carry):
            for m in range(3):
                spread = []
                for a in range(3):
                    force = []
                    for b in range(3):
                        t = 9 * a + 3 * b + c
                        force.append(sum(stress[3 * m + l] * grad[l * 27 + t] for l in range(3)))
                    spread.append(
                        [
                            sum(
                                jnp.where(j_index == y - b, force[b], 0.0)
                                for b in range(3)
                                if 0 <= y - b <= 3
                            )
                            for y in range(6)
                        ]
                    )
                for x in range(6):
                    for y in range(6):
                        row = pl.multiple_of((c * ROWS + (x * 6 + y) * 3 + m) * 8, 8)
                        f_rows[pl.ds(row, 8), :] = sum(
                            jnp.where(i_index == x - a, spread[a][y], 0.0)
                            for a in range(3)
                            if 0 <= x - a <= 3
                        )
            return carry

        lax.fori_loop(0, 3, scatter, 0)
        contract = (((1,), (1,)), ((), ()))
        total = None
        for pair in range(4):
            rows = jnp.concatenate(
                [f_rows[pl.ds(2 * pair + q, 3 * ROWS, stride=8), :] for q in range(2)], axis=1
            )
            mine = hot[:, 2 * pair * LANES : (2 * pair + 2) * LANES]
            high = rows.astype(BF16)
            low = (rows - high.astype(F32)).astype(BF16)
            for value in (high, low):
                term = lax.dot_general(value, mine, contract, preferred_element_type=F32)
                total = term if total is None else total + term
        rows_out[...] = (
            turn(total[0:ROWS], -1) * high_ok[1][0, 0, 0:1]
            + total[ROWS : 2 * ROWS]
            + turn(total[2 * ROWS : 3 * ROWS], 1) * low_ok[1][0, 0, 0:1]
        )
        for n in range(36):
            part[n // 6, n % 6] = rows_out[3 * n : 3 * n + 3, :]
        part[1:5, 1:5] = part[1:5, 1:5] + mass[3:7, 3:7] * field[1:5, 1:5]

    def fine_residual(rhs):
        e0_ref[...] = inv0[...] * rhs[...]
        return (
            0.3 * rhs[1:9, 1:9]
            + e0_ref[0:8, 1:9]
            + e0_ref[2:10, 1:9]
            + e0_ref[1:9, 0:8]
            + e0_ref[1:9, 2:10]
            + beside_z(e0_ref[1:9, 1:9], 1)
        )

    def far_start(turn_no):
        far_own = (far_own0, far_own1)[turn_no]
        far_slots = (far_in0, far_in1)[turn_no]
        for dx, dy in FAR:
            copy = pltpu.make_async_remote_copy(
                src_ref=far_own,
                dst_ref=far_slots.at[(4 - dx) * 9 + 4 - dy],
                send_sem=far_send.at[turn_no],
                recv_sem=far_recv.at[turn_no],
                device_id=device(dx, dy),
                device_id_type=MESH,
            )
            copy.start()

    def one_start(turn_no):
        for i, d in enumerate(NEAR):
            one_own = (one_own0, one_own1)[turn_no]
            send(one_own, one_in[turn_no][other(d)], 1 + turn_no, i, d)

    def first_half():
        b1 = coarser(fine_residual(rhs0), 1)
        mass1 = coarser(jnp.broadcast_to(mass[1:9, 1:9], (8, 8, 3, LANES)), 1)
        inv1 = 0.7 / (mass1 + 12.0)
        one_inv[1:5, 1:5] = inv1
        one_inv[1:2, 1:5] = one_inv[1:2, 1:5] * inside[0][0]
        one_inv[4:5, 1:5] = one_inv[4:5, 1:5] * inside[0][1]
        one_inv[1:5, 1:2] = one_inv[1:5, 1:2] * inside[1][0]
        one_inv[1:5, 4:5] = one_inv[1:5, 4:5] * inside[1][1]
        e1 = one_inv[1:5, 1:5] * b1
        r1 = 0.3 * b1[1:3, 1:3] + 2.0 * (
            e1[0:2, 1:3] + e1[2:4, 1:3] + e1[1:3, 0:2] + e1[1:3, 2:4] + beside_z(e1[1:3, 1:3], 2)
        )
        b2 = coarser(r1, 2)[0, 0]
        mass2 = coarser(mass1[1:3, 1:3], 2)[0, 0]
        far_own0[...] = (
            jnp.sum(b2 * pack_mask, axis=0, keepdims=True) + mass2[0:1] * mass_mask
        )
        far_start(0)
        one_own0[:, :, 0:3, :] = b1[1:3, 1:3]
        one_own0[:, :, 3:4, :] = mass1[1:3, 1:3, 0:1]
        one_start(0)
        for pad in (fine_pad, one_pad, one_share, rhs1):
            pad[...] = jnp.zeros_like(pad)

    def own_share():
        est = inv0[2:8, 2:8] * part0[...]
        e0_ref[2:8, 2:8] = est
        fine_pad[1:7, 1:7] = (
            0.3 * part0[...]
            + e0_ref[1:7, 2:8]
            + e0_ref[3:9, 2:8]
            + e0_ref[2:8, 1:7]
            + e0_ref[2:8, 3:9]
            + beside_z(est, 1)
        )
        fine_pad[0:1, 1:7] = est[0:1]
        fine_pad[7:8, 1:7] = est[5:6]
        fine_pad[1:7, 0:1] = est[:, 0:1]
        fine_pad[1:7, 7:8] = est[:, 5:6]
        b1 = coarser(fine_pad[...], 1)
        est = one_inv[1:5, 1:5] * b1
        one_pad[1:5, 1:5] = est
        one_share[1:5, 1:5] = 0.3 * b1 + 2.0 * (
            one_pad[0:4, 1:5]
            + one_pad[2:6, 1:5]
            + one_pad[1:5, 0:4]
            + one_pad[1:5, 2:6]
            + beside_z(est, 2)
        )
        one_share[0:1, 1:5] = 2.0 * est[0:1]
        one_share[5:6, 1:5] = 2.0 * est[3:4]
        one_share[1:5, 0:1] = 2.0 * est[:, 0:1]
        one_share[1:5, 5:6] = 2.0 * est[:, 3:4]
        r1 = one_share[...]
        b2 = coarser(r1, 2)
        for x in range(3):
            for y in range(3):
                few_out[3 * x + y] = jnp.sum(b2[x, y] * pack_mask, axis=0, keepdims=True)

    def second_half(turn_no, rhs, field):
        far_own = (far_own0, far_own1)[turn_no]
        far_slots = (far_in0, far_in1)[turn_no]
        one_own = (one_own0, one_own1)[turn_no]
        one_rhs[2:4, 2:4] = one_own[:, :, 0:3, :]
        for i, d in enumerate(NEAR):
            got = one_in[turn_no][i]
            arrived(got, 1 + turn_no, i)
            sx, sy = slice(2 + 2 * d[0], 4 + 2 * d[0]), slice(2 + 2 * d[1], 4 + 2 * d[1])
            one_rhs[sx, sy] = got[:, :, 0:3, :]
            if turn_no == 0:
                keep = jnp.float32(1.0)
                if d[0]:
                    keep = keep * inside[0][(d[0] + 1) // 2]
                if d[1]:
                    keep = keep * inside[1][(d[1] + 1) // 2]
                beside = jnp.broadcast_to(got[:, :, 3:4, :], (2, 2, 3, LANES))
                one_inv[sx, sy] = (0.7 / (beside + 12.0)) * keep
        far_all = far_slots.at[pl.ds(0, len(FAR))]
        closers.append((far_all, far_send.at[turn_no]))
        pltpu.make_async_copy(far_all, far_all, far_recv.at[turn_no]).wait()
        for dx, dy in FAR:
            far_rhs[dx + 4, dy + 4 : dy + 5, :] = far_slots[(dx + 4) * 9 + dy + 4]
        far_rhs[4, 4:5, :] = far_own[...]
        b = far_rhs[...]
        if turn_no == 0:
            quarter = lax.broadcasted_iota(jnp.int32, b.shape, 2) & 3
            diagonal = jnp.where(
                quarter == 0, turn(b, -3), jnp.where(quarter == 1, turn(b, -2), turn(b, -1))
            )
            at_x = lax.broadcasted_iota(jnp.int32, b.shape, 0) + (gx - 4)
            at_y = lax.broadcasted_iota(jnp.int32, b.shape, 1) + (gy - 4)
            within = (at_x >= 0) & (at_x < n_gx) & (at_y >= 0) & (at_y < n_gy)
            far_inv[...] = jnp.where(within, 0.7 / (diagonal + 24.0), 0.0)
        est = far_inv[...] * b
        for sweep in range(3):
            lo, hi = sweep + 1, 8 - sweep
            mid = est[1:-1]
            near = est[:-2] + est[2:] + pltpu.roll(mid, 1, 1) + pltpu.roll(mid, 15, 1)
            near = near + turn(mid, 4) * low_ok[4][0, :, 0:1] + turn(mid, -4) * high_ok[4][0, :, 0:1]
            est = 0.3 * mid + far_inv[lo:hi] * (b[lo:hi] + 4.0 * near)
        far_est[...] = est
        b1 = one_rhs[...]
        inv1 = one_inv[...]
        e2 = jnp.stack(
            [
                jnp.stack(
                    [
                        jnp.take_along_axis(
                            jnp.broadcast_to(far_est[x, 3 + y : 4 + y, :], (8, LANES)),
                            unpack_index,
                            axis=1,
                            mode="promise_in_bounds",
                        )[0:3]
                        for y in range(3)
                    ]
                )
                for x in range(3)
            ]
        )
        e1 = inv1 * b1 + finer(e2)
        mid = e1[1:5, 1:5]
        near = e1[0:4, 1:5] + e1[2:6, 1:5] + e1[1:5, 0:4] + e1[1:5, 2:6] + beside_z(mid, 2)
        e1 = 0.3 * mid + inv1[1:5, 1:5] * (b1[1:5, 1:5] + 2.0 * near)
        e0 = e0_ref[1:9, 1:9] + finer(e1)
        mid = e0[1:7, 1:7]
        near = e0[0:6, 1:7] + e0[2:8, 1:7] + e0[1:7, 0:6] + e0[1:7, 2:8] + beside_z(mid, 1)
        field[...] = 0.3 * mid + inv0[2:8, 2:8] * (rhs[2:8, 2:8] + near)

    def down(v):
        return jnp.sum(v.sum(axis=(0, 1)), axis=0, keepdims=True)

    def early_sums():
        sums[...] = jnp.zeros_like(sums)
        sums[0:1] = down(rhs0[3:7, 3:7] * z_ref[1:5, 1:5])
        sums[1:2] = down(rhs1[3:7, 3:7] * z_ref[1:5, 1:5])

    for i, d in enumerate(NEAR):
        got = first_in[i]
        arrived(got, 0, i)
        sx, sy = box(first_place, d)
        rhs0[sx, sy] = got[:, :, 0:3, :]
        mass[sx, sy] = got[:, :, 3:4, :]
    for x in range(10):
        for y in range(10):
            mass_rows[x, y : y + 1, :] = mass[x, y]
    at_x = lax.broadcasted_iota(jnp.int32, (10, 16, LANES), 0) + (gx * 4 - 3)
    at_y = lax.broadcasted_iota(jnp.int32, (10, 16, LANES), 1) + (gy * 4 - 3)
    within = (at_x >= 0) & (at_x < 4 * n_gx) & (at_y >= 0) & (at_y < 4 * n_gy)
    inv_rows[...] = jnp.where(within, 0.7 / (mass_rows[...] + 6.0), 0.0)
    for x in range(10):
        for y in range(10):
            inv0[x, y] = jnp.broadcast_to(inv_rows[x, y : y + 1, :], (3, LANES))
    first_half()
    second_half(0, rhs0, z_ref)
    for x in (1, 8):
        e0_ref[x : x + 1, 1:9] = jnp.zeros((1, 8, 3, LANES), F32)
        e0_ref[1:9, x : x + 1] = jnp.zeros((8, 1, 3, LANES), F32)
    stress, _ = strains(z_ref)
    forces(stress, z_ref, part0)

    def kept(d):
        keep = jnp.bool_(True)
        if d[0]:
            keep = keep & ((gx > 0) if d[0] < 0 else (gx < n_gx - 1))
        if d[1]:
            keep = keep & ((gy > 0) if d[1] < 0 else (gy < n_gy - 1))
        return jnp.where(keep, 1.0, 0.0).astype(F32)

    own_share()
    for i, d in enumerate(NEAR):
        send(few_out.at[3 * d[0] + d[1] + 4], few_in.at[other(d)], 5, i, d)
    for i, d in enumerate(NEAR):
        if d[0] and d[1]:
            n = (2, 3, 4, 5).index(i)
            for k, (p, q) in enumerate(CORNER):
                corner_out[n, k] = part0[5 - p if d[0] > 0 else p, 5 - q if d[1] > 0 else q]
            send(corner_out.at[n], wide_in[other(d)], 3, i, d)
        else:
            sx, sy = box(wide_cut, d)
            send(part0.at[sx, sy], wide_in[other(d)], 3, i, d)
    rhs1[2:8, 2:8] = part0[...]
    coarse = few_out[4]
    for i, d in enumerate(NEAR):
        arrived(few_in.at[i], 5, i)
        coarse = coarse + few_in[i] * kept(d)
    far_own1[...] = coarse
    far_start(1)
    for i, d in enumerate(NEAR):
        got = wide_in[i]
        arrived(got, 3, i)
        if d[0] and d[1]:
            for k, (p, q) in enumerate(CORNER):
                x, y = (3 - p if d[0] < 0 else 6 + p), (3 - q if d[1] < 0 else 6 + q)
                rhs1[x, y] = rhs1[x, y] + got[k] * kept(d)
        else:
            sx, sy = box(wide_place, d)
            rhs1[sx, sy] = rhs1[sx, sy] + got[...] * kept(d)
    e0_ref[1:9, 1:9] = inv0[1:9, 1:9] * rhs1[1:9, 1:9]
    r0 = (
        0.3 * rhs1[3:7, 3:7]
        + e0_ref[2:6, 3:7]
        + e0_ref[4:8, 3:7]
        + e0_ref[3:7, 2:6]
        + e0_ref[3:7, 4:8]
        + beside_z(e0_ref[3:7, 3:7], 1)
    )
    one_own1[...] = coarser(r0, 1)
    one_start(1)
    early_sums()
    second_half(1, rhs1, u_ref)
    stress, energy = strains(u_ref)

    def line_start(src, slots, stage, count, step):
        for d in range(1, count):
            copy = pltpu.make_async_remote_copy(
                src_ref=src,
                dst_ref=slots.at[d - 1],
                send_sem=line_send.at[stage],
                recv_sem=line_recv.at[stage],
                device_id=device(*step(d)),
                device_id_type=MESH,
            )
            copy.start()
        closers.append((slots.at[pl.ds(0, count - 1)], line_send.at[stage]))

    def line_end(src, slots, stage, count):
        whole = slots.at[pl.ds(0, count - 1)]
        pltpu.make_async_copy(whole, whole, line_recv.at[stage]).wait()
        total = src[...]
        for d in range(1, count):
            total = total + slots[d - 1]
        return total

    b = rhs0[3:7, 3:7]
    w = rhs1[3:7, 3:7]
    z = z_ref[1:5, 1:5]
    u = u_ref[1:5, 1:5]
    own_mass = jnp.broadcast_to(mass[3:7, 3:7], z.shape)
    sums[2:3] = down(b * u)
    sums[3:4] = down(w * u)
    sums[4:5] = down(own_mass * u * u) + jnp.sum(energy, axis=0, keepdims=True)
    across = jnp.broadcast_to(jnp.sum(sums[...], axis=1, keepdims=True), (8, LANES))
    sum_own[...] = jnp.sum(jnp.where(lane2 == sub2, across, 0.0), axis=0, keepdims=True)
    line_start(sum_own, line_in, 0, n_gx, lambda d: ((16 + d) % n_gx if d != 16 else 16, 0))
    forces(stress, u_ref, part1)
    for i, d in enumerate(NEAR):
        sx, sy = box(thin_cut, d)
        send(part1.at[sx, sy], thin_in[other(d)], 4, i, d)
    sum_own2[...] = line_end(sum_own, line_in, 0, n_gx)
    line_start(sum_own2, line_in2, 1, n_gy, lambda d: (0, (8 + d) % n_gy if d != 8 else 8))
    total = line_end(sum_own2, line_in2, 1, n_gy)

    def scalar(i):
        index = jnp.full((8, LANES), i, jnp.int32)
        return jnp.take_along_axis(
            jnp.broadcast_to(total, (8, LANES)), index, axis=1, mode="promise_in_bounds"
        )

    bz, zw, bu, wu, uv = (scalar(i) for i in range(5))
    step0 = bz / zw
    rz1 = bz - step0 * (bu + zw) + step0 * step0 * wu
    ratio = rz1 / bz
    mixed = zw - step0 * wu
    curve = zw - 2.0 * step0 * wu + step0 * step0 * uv + 2.0 * ratio * mixed + ratio * ratio * zw
    step1 = rz1 / curve
    first = (step0 + step1 + step1 * ratio)[0:3]
    second = (step1 * step0)[0:3]

    answer[...] = first * z - second * u
    for n in range(48):
        x, y, m = n // 12, n // 3 % 4, n % 3
        x_ref[m, x, y : y + 1, :] = answer[x, y, m : m + 1, :]
    e0_ref[0:4, 0:4] = part1[1:5, 1:5]
    for i, d in enumerate(NEAR):
        arrived(thin_in[i], 4, i)
        sx, sy = box(thin_place, d)
        e0_ref[sx, sy] = e0_ref[sx, sy] + thin_in[i][...] * kept(d)
    answer[...] = b - first * w + second * e0_ref[0:4, 0:4]
    for n in range(48):
        x, y, m = n // 12, n // 3 % 4, n % 3
        r_ref[m, x, y : y + 1, :] = answer[x, y, m : m + 1, :]
    close()


def solution(mesh):
    n_gx, n_gy = mesh.shape["gx"], mesh.shape["gy"]

    def vmem(*shape, dtype=F32):
        return pltpu.VMEM(shape, dtype)

    scratch = [vmem(*extent(first_cut, (-d[0], -d[1]), 4)) for d in NEAR]
    scratch += [
        vmem(len(CORNER), 3, LANES) if d[0] and d[1] else vmem(*extent(wide_cut, (-d[0], -d[1]), 3))
        for d in NEAR
    ]
    scratch += [vmem(*extent(thin_cut, (-d[0], -d[1]), 3)) for d in NEAR]
    scratch += [vmem(2, 2, 4, LANES) for _ in range(8)]
    scratch += [vmem(2, 2, 3, LANES) for _ in range(8)]
    scratch += [
        vmem(3, 4, 4, LANES), vmem(4, 4, LANES),
        vmem(8, LANES), vmem(8, LANES, dtype=jnp.int32), vmem(8, LANES, dtype=jnp.int32),
    ]
    scratch += [
        vmem(81, 8, LANES),
        vmem(4, 4, 4, LANES),
        vmem(10, 10, 3, LANES),
        vmem(10, 10, 3, LANES),
        vmem(10, 10, 1, LANES),
        vmem(10, 10, 3, LANES),
        vmem(10, 10, 3, LANES),
        vmem(2, 2, 4, LANES),
        vmem(2, 2, 3, LANES),
        vmem(6, 6, 3, LANES),
        vmem(6, 6, 3, LANES),
        vmem(1, LANES),
        vmem(1, LANES),
        vmem(81, 1, LANES),
        vmem(81, 1, LANES),
        vmem(9, 16, LANES),
        vmem(9, 16, LANES),
        vmem(3, 16, LANES),
        vmem(6, 6, 3, LANES),
        vmem(6, 6, 3, LANES),
        vmem(3, 6, 6, 3, LANES),
        vmem(3 * ROWS * 8, LANES),
        vmem(LANES, 8 * LANES, dtype=BF16),
        vmem(ROWS, LANES),
        vmem(6, 6, 3, LANES),
        vmem(6, 6, 3, LANES),
        vmem(8, LANES),
        vmem(1, LANES),
        vmem(1, LANES),
        vmem(n_gx, 1, LANES),
        vmem(n_gy, 1, LANES),
        vmem(4, 4, 3, LANES),
        vmem(4, len(CORNER), 3, LANES),
        vmem(9, 1, LANES),
        vmem(8, 1, LANES),
        vmem(6, 6, 3, LANES),
        vmem(8, 8, 3, LANES),
        vmem(6, 6, 3, LANES),
        vmem(10, 16, LANES),
        vmem(10, 16, LANES),
        pltpu.SemaphoreType.DMA((6, 8)),
        pltpu.SemaphoreType.DMA((6, 8)),
        pltpu.SemaphoreType.DMA((2,)),
        pltpu.SemaphoreType.DMA((2,)),
        pltpu.SemaphoreType.DMA((2,)),
        pltpu.SemaphoreType.DMA((2,)),
        pltpu.SemaphoreType.DMA((6,)),
    ]

    def body(right, mass, gradients, *rest):
        by_tile = jnp.transpose(gradients[0, 0], (1, 2, 0, 3)).reshape(81, 8, LANES)
        args = (right, mass, by_tile) + rest
        call = pl.pallas_call(
            lambda *refs: kernel(n_gx, n_gy, *refs),
            out_shape=[pltpu.VMEM((3, 4, 4, LANES), F32)] * 2,
            in_specs=[pl.BlockSpec(memory_space=pl.ANY)] * 6,
            out_specs=[pl.BlockSpec(memory_space=pltpu.VMEM)] * 2,
            scratch_shapes=scratch,
            compiler_params=pltpu.CompilerParams(collective_id=0, has_side_effects=True),
            name="cg",
        )
        return tuple(call(*args))

    field = P(None, "gx", "gy", None)
    block = P("gx", "gy", None, None)
    return jax.shard_map(
        body,
        mesh=mesh,
        in_specs=(field, P("gx", "gy", None), P("gx", "gy", None, None, None, None)) + (block,) * 3,
        out_specs=(field, field),
        check_vma=False,
    )
```

```python
import jax
import jax.numpy as jnp
from jax import lax
from jax.experimental import pallas as pl
from jax.experimental.pallas import tpu as pltpu
from jax.sharding import PartitionSpec as P

MESH = pl.DeviceIdType.MESH
F32 = jnp.float32
BF16 = jnp.bfloat16
LANES = 128
POISSON = 0.3
NEAR = tuple(
    (dx, dy)
    for dx, dy in ((0, 1), (0, -1), (1, 1), (1, -1), (-1, 1), (-1, -1), (1, 0), (-1, 0))
)
DIAGONAL_FIRST = tuple(sorted(enumerate(NEAR), key=lambda e: -abs(e[1][0]) - abs(e[1][1])))
FAR = tuple(
    sorted(
        (
            (dx, dy)
            for dx in range(-4, 5)
            for dy in range(-4, 5)
            if (dx, dy) != (0, 0) and max(abs(dx) - 1, 0) + max(abs(dy) - 1, 0) <= 3
        ),
        key=lambda d: (-abs(d[1]) - (0, 2, 2, 3, 3)[abs(d[0])], -abs(d[1])),
    )
)
GREETED = tuple(
    (dx, dy)
    for dx in range(-3, 4)
    for dy in range(-3, 4)
    if 0 < abs(dx) + abs(dy) <= 3
) + tuple((d, 0) for d in (14, 15, 16, -15, -14))
CORNER = tuple((p, q) for p in range(3) for q in range(3) if p + q <= 3)
ROWS = 112


def farthest(n):
    return sorted(range(1, n), key=lambda d: (-min(d, n - d), d))


def first_cut(d, diagonal):
    if d == 0:
        return (0, 4)
    wide = 2 if diagonal else 3
    return (4 - wide, 4) if d > 0 else (0, wide)


def first_place(d, diagonal):
    if d == 0:
        return (3, 7)
    wide = 2 if diagonal else 3
    return (7, 7 + wide) if d > 0 else (3 - wide, 3)


def wide_cut(d, diagonal):
    return ((0, 3), (0, 6), (3, 6))[d + 1]


def wide_place(d, diagonal):
    return ((1, 4), (2, 8), (6, 9))[d + 1]


def thin_cut(d, diagonal):
    return ((0, 1), (1, 5), (5, 6))[d + 1]


def thin_place(d, diagonal):
    return ((0, 1), (0, 4), (3, 4))[d + 1]


def box(cut, d):
    diagonal = d[0] != 0 and d[1] != 0
    (x0, x1), (y0, y1) = cut(d[0], diagonal), cut(d[1], diagonal)
    return slice(x0, x1), slice(y0, y1)


def extent(cut, d, rows):
    sx, sy = box(cut, d)
    return (sx.stop - sx.start, sy.stop - sy.start, rows, LANES)


def kernel(n_gx, n_gy, *refs):
    (b_hbm, m_hbm, g_hbm, s_hbm, v_hbm, n_hbm, both_ref), refs = refs[:7], refs[7:]
    x_ref, r_ref = both_ref.at[0], both_ref.at[1]
    first_in, wide_in, thin_in = refs[:8], refs[8:16], refs[16:24]
    one_in = (refs[24:32], refs[32:40])
    (b_in, m_in, s_in, v_in, n_in), refs = refs[40:45], refs[45:]
    (
        grad, own, rhs0, rhs1, mass, inv0, e0_ref, one_own0, one_own1, one_rhs, one_inv,
        far_own0, far_own1, far_in0, far_in1, far_rhs, far_inv, far_est, z_ref, u_ref,
        z_shift, f_rows, hot, rows_out, part0, part1, sums, sum_own,
        sum_own2, line_in, line_in2, answer, corner_out, few_out, few_in, one_pad, fine_pad, one_share, mass_rows, inv_rows, near_send, near_recv, far_send, far_recv,
        line_send, line_recv, local_sem,
    ) = refs

    gx, gy = lax.axis_index("gx"), lax.axis_index("gy")

    def device(dx, dy):
        return {"gx": lax.rem(gx + (dx % n_gx), n_gx), "gy": lax.rem(gy + (dy % n_gy), n_gy)}

    loads = [
        pltpu.make_async_copy(src, dst, local_sem.at[i])
        for i, (src, dst) in enumerate(
            (
                (b_hbm, b_in), (m_hbm, m_in), (g_hbm, grad),
                (s_hbm.at[0, 0], s_in), (v_hbm.at[0, 0], v_in), (n_hbm.at[0, 0], n_in),
            )
        )
    ]
    for load in loads:
        load.start()
    partners = list(NEAR) + sorted(set(GREETED) - set(NEAR))
    barrier = pltpu.get_barrier_semaphore()
    for dx, dy in partners:
        pl.semaphore_signal(barrier, inc=1, device_id=device(dx, dy), device_id_type=MESH)
    for load in (loads[0], loads[1]):
        load.wait()
    for x in range(4):
        for y in range(4):
            for m in range(3):
                own[x, y, m : m + 1, :] = b_in[m, x, y : y + 1, :]
            own[x, y, 3:4, :] = m_in[x, y : y + 1, :]
    rhs0[3:7, 3:7] = own[:, :, 0:3, :]
    mass[3:7, 3:7] = own[:, :, 3:4, :]

    pl.semaphore_wait(barrier, len(partners))

    started = []
    closers = []

    def close():
        for copy in started:
            copy.wait_send()
        for whole, sem in closers:
            pltpu.make_async_copy(whole, whole, sem).wait()

    def send(src, dst, group, i, d):
        copy = pltpu.make_async_remote_copy(
            src_ref=src,
            dst_ref=dst,
            send_sem=near_send.at[group, i],
            recv_sem=near_recv.at[group, NEAR.index((-d[0], -d[1]))],
            device_id=device(*d),
            device_id_type=MESH,
        )
        copy.start()
        started.append(copy)

    def arrived(dst, group, i):
        pltpu.make_async_copy(dst, dst, near_recv.at[group, i]).wait()

    def other(d):
        return NEAR.index((-d[0], -d[1]))

    for i, d in DIAGONAL_FIRST:
        sx, sy = box(first_cut, d)
        send(own.at[sx, sy], first_in[other(d)], 0, i, d)

    lane4 = lax.broadcasted_iota(jnp.int32, (1, 1, 3, LANES), 3)

    def ones_where(cond):
        return jnp.where(cond, 1.0, 0.0).astype(F32)

    low_ok = {s: ones_where(lane4 >= s) for s in (1, 2, 4)}
    high_ok = {s: ones_where(lane4 < LANES - s) for s in (1, 2, 4)}
    odd = {s: ones_where((lane4 & s) != 0) for s in (1, 2)}
    even = {s: ones_where((lane4 & s) == 0) for s in (1, 2)}

    def turn(v, s):
        return pltpu.roll(v, s % LANES, v.ndim - 1)

    def beside_z(v, s):
        return turn(v, s) * low_ok[s] + turn(v, -s) * high_ok[s]

    def pair_z(v, s):
        return v + turn(v, s) * odd[s] + turn(v, -s) * even[s]

    def coarser(v, s):
        nx, ny = v.shape[0] // 2, v.shape[1] // 2
        w = v.reshape((nx, 2, ny, 2) + v.shape[2:])
        w = (w[:, 0] + w[:, 1])
        w = w[:, :, 0] + w[:, :, 1]
        return pair_z(w, s)

    def finer(v):
        nx, ny = v.shape[:2]
        w = jnp.broadcast_to(v[:, None, :, None], (nx, 2, ny, 2) + v.shape[2:])
        return w.reshape((2 * nx, 2 * ny) + v.shape[2:])

    lane2 = lax.broadcasted_iota(jnp.int32, (8, LANES), 1)
    sub2 = lax.broadcasted_iota(jnp.int32, (8, LANES), 0)
    pack_mask = ones_where((lane2 & 3) == sub2)[0:3]
    mass_mask = ones_where((lane2 & 3) == 3)[0:1]
    unpack_index = (lane2 & ~3) + jnp.minimum(sub2, 2)
    inside = (
        (ones_where(gx > 0), ones_where(gx < n_gx - 1)),
        (ones_where(gy > 0), ones_where(gy < n_gy - 1)),
    )

    for load in loads[2:]:
        load.wait()
    node = n_in[...]
    quotient = (node * 2017) >> 18
    k_index = node - quotient * 130
    i_index = (quotient * 43) >> 8
    j_index = quotient - i_index * 6
    effective = s_in[...] * v_in[...].astype(F32)
    z_rows = lax.broadcasted_iota(jnp.int32, (LANES, LANES), 0)
    for s in range(8):
        same = jnp.broadcast_to(k_index[s : s + 1, :], (LANES, LANES)) == z_rows
        hot[:, s * LANES : (s + 1) * LANES] = ones_where(same).astype(BF16)
    shear = effective * (0.5 / (1.0 + POISSON))
    lame = effective * (POISSON / ((1.0 + POISSON) * (1.0 - 2.0 * POISSON)))

    def strains(field):
        v = field[...]
        z_shift[0] = turn(v, 1) * low_ok[1]
        z_shift[1] = v
        z_shift[2] = turn(v, -1) * high_ok[1]
        i_lo, i_hi = (i_index & 1) != 0, (i_index & 2) != 0
        j_lo, j_hi = (j_index & 1) != 0, (j_index & 2) != 0

        def four(v0, v1, v2, v3, lo, hi):
            return jnp.where(hi, jnp.where(lo, v3, v2), jnp.where(lo, v1, v0))

        def gather(c, disp):
            disp = list(disp)
            for m in range(3):
                picked = [
                    [
                        jnp.take_along_axis(
                            jnp.broadcast_to(z_shift[c, x, y, m : m + 1, :], (8, LANES)),
                            k_index,
                            axis=1,
                            mode="promise_in_bounds",
                        )
                        for y in range(6)
                    ]
                    for x in range(6)
                ]
                for a in range(3):
                    row = [
                        four(*(picked[a + i][y] for i in range(4)), i_lo, i_hi) for y in range(6)
                    ]
                    for b in range(3):
                        value = four(*row[b : b + 4], j_lo, j_hi)
                        for l in range(3):
                            at = grad[l * 27 + 9 * a + 3 * b + c]
                            disp[3 * m + l] = disp[3 * m + l] + value * at
            return tuple(disp)

        zero = jnp.zeros((8, LANES), F32)
        disp = lax.fori_loop(0, 3, gather, (zero,) * 9)
        trace = lame * (disp[0] + disp[4] + disp[8])
        stress = [
            shear * (disp[3 * m + l] + disp[3 * l + m]) + (trace if m == l else 0.0)
            for m in range(3)
            for l in range(3)
        ]
        return stress, sum(stress[q] * disp[q] for q in range(9))

    def forces(stress, field, part):
        def scatter(c, carry):
            for m in range(3):
                spread = []
                for a in range(3):
                    force = []
                    for b in range(3):
                        t = 9 * a + 3 * b + c
                        force.append(sum(stress[3 * m + l] * grad[l * 27 + t] for l in range(3)))
                    spread.append(
                        [
                            sum(
                                jnp.where(j_index == y - b, force[b], 0.0)
                                for b in range(3)
                                if 0 <= y - b <= 3
                            )
                            for y in range(6)
                        ]
                    )
                for x in range(6):
                    for y in range(6):
                        row = pl.multiple_of((c * ROWS + (x * 6 + y) * 3 + m) * 8, 8)
                        f_rows[pl.ds(row, 8), :] = sum(
                            jnp.where(i_index == x - a, spread[a][y], 0.0)
                            for a in range(3)
                            if 0 <= x - a <= 3
                        )
            return carry

        lax.fori_loop(0, 3, scatter, 0)
        contract = (((1,), (1,)), ((), ()))
        total = None
        for pair in range(4):
            rows = jnp.concatenate(
                [f_rows[pl.ds(2 * pair + q, 3 * ROWS, stride=8), :] for q in range(2)], axis=1
            )
            mine = hot[:, 2 * pair * LANES : (2 * pair + 2) * LANES]
            high = rows.astype(BF16)
            low = (rows - high.astype(F32)).astype(BF16)
            for value in (high, low):
                term = lax.dot_general(value, mine, contract, preferred_element_type=F32)
                total = term if total is None else total + term
        rows_out[...] = (
            turn(total[0:ROWS], -1) * high_ok[1][0, 0, 0:1]
            + total[ROWS : 2 * ROWS]
            + turn(total[2 * ROWS : 3 * ROWS], 1) * low_ok[1][0, 0, 0:1]
        )
        for n in range(36):
            part[n // 6, n % 6] = rows_out[3 * n : 3 * n + 3, :]
        part[1:5, 1:5] = part[1:5, 1:5] + mass[3:7, 3:7] * field[1:5, 1:5]

    def fine_residual(rhs):
        e0_ref[...] = inv0[...] * rhs[...]
        return (
            0.3 * rhs[1:9, 1:9]
            + e0_ref[0:8, 1:9]
            + e0_ref[2:10, 1:9]
            + e0_ref[1:9, 0:8]
            + e0_ref[1:9, 2:10]
            + beside_z(e0_ref[1:9, 1:9], 1)
        )

    def far_start(turn_no):
        far_own = (far_own0, far_own1)[turn_no]
        far_slots = (far_in0, far_in1)[turn_no]
        for dx, dy in FAR:
            copy = pltpu.make_async_remote_copy(
                src_ref=far_own,
                dst_ref=far_slots.at[(4 - dx) * 9 + 4 - dy],
                send_sem=far_send.at[turn_no],
                recv_sem=far_recv.at[turn_no],
                device_id=device(dx, dy),
                device_id_type=MESH,
            )
            copy.start()

    def one_start(turn_no):
        for i, d in enumerate(NEAR):
            one_own = (one_own0, one_own1)[turn_no]
            send(one_own, one_in[turn_no][other(d)], 1 + turn_no, i, d)

    def first_half():
        b1 = coarser(fine_residual(rhs0), 1)
        mass1 = coarser(jnp.broadcast_to(mass[1:9, 1:9], (8, 8, 3, LANES)), 1)
        inv1 = 0.7 / (mass1 + 12.0)
        one_inv[1:5, 1:5] = inv1
        one_inv[1:2, 1:5] = one_inv[1:2, 1:5] * inside[0][0]
        one_inv[4:5, 1:5] = one_inv[4:5, 1:5] * inside[0][1]
        one_inv[1:5, 1:2] = one_inv[1:5, 1:2] * inside[1][0]
        one_inv[1:5, 4:5] = one_inv[1:5, 4:5] * inside[1][1]
        e1 = one_inv[1:5, 1:5] * b1
        r1 = 0.3 * b1[1:3, 1:3] + 2.0 * (
            e1[0:2, 1:3] + e1[2:4, 1:3] + e1[1:3, 0:2] + e1[1:3, 2:4] + beside_z(e1[1:3, 1:3], 2)
        )
        b2 = coarser(r1, 2)[0, 0]
        mass2 = coarser(mass1[1:3, 1:3], 2)[0, 0]
        far_own0[...] = (
            jnp.sum(b2 * pack_mask, axis=0, keepdims=True) + mass2[0:1] * mass_mask
        )
        far_start(0)
        one_own0[:, :, 0:3, :] = b1[1:3, 1:3]
        one_own0[:, :, 3:4, :] = mass1[1:3, 1:3, 0:1]
        one_start(0)
        for pad in (fine_pad, one_pad, one_share, rhs1):
            pad[...] = jnp.zeros_like(pad)

    def own_share():
        est = inv0[2:8, 2:8] * part0[...]
        e0_ref[2:8, 2:8] = est
        fine_pad[1:7, 1:7] = (
            0.3 * part0[...]
            + e0_ref[1:7, 2:8]
            + e0_ref[3:9, 2:8]
            + e0_ref[2:8, 1:7]
            + e0_ref[2:8, 3:9]
            + beside_z(est, 1)
        )
        fine_pad[0:1, 1:7] = est[0:1]
        fine_pad[7:8, 1:7] = est[5:6]
        fine_pad[1:7, 0:1] = est[:, 0:1]
        fine_pad[1:7, 7:8] = est[:, 5:6]
        b1 = coarser(fine_pad[...], 1)
        est = one_inv[1:5, 1:5] * b1
        one_pad[1:5, 1:5] = est
        one_share[1:5, 1:5] = 0.3 * b1 + 2.0 * (
            one_pad[0:4, 1:5]
            + one_pad[2:6, 1:5]
            + one_pad[1:5, 0:4]
            + one_pad[1:5, 2:6]
            + beside_z(est, 2)
        )
        one_share[0:1, 1:5] = 2.0 * est[0:1]
        one_share[5:6, 1:5] = 2.0 * est[3:4]
        one_share[1:5, 0:1] = 2.0 * est[:, 0:1]
        one_share[1:5, 5:6] = 2.0 * est[:, 3:4]
        r1 = one_share[...]
        b2 = coarser(r1, 2)
        for x in range(3):
            for y in range(3):
                few_out[3 * x + y] = jnp.sum(b2[x, y] * pack_mask, axis=0, keepdims=True)

    def second_half(turn_no, rhs, field):
        far_own = (far_own0, far_own1)[turn_no]
        far_slots = (far_in0, far_in1)[turn_no]
        one_own = (one_own0, one_own1)[turn_no]
        one_rhs[2:4, 2:4] = one_own[:, :, 0:3, :]
        for i, d in enumerate(NEAR):
            got = one_in[turn_no][i]
            arrived(got, 1 + turn_no, i)
            sx, sy = slice(2 + 2 * d[0], 4 + 2 * d[0]), slice(2 + 2 * d[1], 4 + 2 * d[1])
            one_rhs[sx, sy] = got[:, :, 0:3, :]
            if turn_no == 0:
                keep = jnp.float32(1.0)
                if d[0]:
                    keep = keep * inside[0][(d[0] + 1) // 2]
                if d[1]:
                    keep = keep * inside[1][(d[1] + 1) // 2]
                beside = jnp.broadcast_to(got[:, :, 3:4, :], (2, 2, 3, LANES))
                one_inv[sx, sy] = (0.7 / (beside + 12.0)) * keep
        far_all = far_slots.at[pl.ds(0, len(FAR))]
        closers.append((far_all, far_send.at[turn_no]))
        pltpu.make_async_copy(far_all, far_all, far_recv.at[turn_no]).wait()
        for dx, dy in FAR:
            far_rhs[dx + 4, dy + 4 : dy + 5, :] = far_slots[(dx + 4) * 9 + dy + 4]
        far_rhs[4, 4:5, :] = far_own[...]
        b = far_rhs[...]
        if turn_no == 0:
            quarter = lax.broadcasted_iota(jnp.int32, b.shape, 2) & 3
            diagonal = jnp.where(
                quarter == 0, turn(b, -3), jnp.where(quarter == 1, turn(b, -2), turn(b, -1))
            )
            at_x = lax.broadcasted_iota(jnp.int32, b.shape, 0) + (gx - 4)
            at_y = lax.broadcasted_iota(jnp.int32, b.shape, 1) + (gy - 4)
            within = (at_x >= 0) & (at_x < n_gx) & (at_y >= 0) & (at_y < n_gy)
            far_inv[...] = jnp.where(within, 0.7 / (diagonal + 24.0), 0.0)
        est = far_inv[...] * b
        for sweep in range(3):
            lo, hi = sweep + 1, 8 - sweep
            mid = est[1:-1]
            near = est[:-2] + est[2:] + pltpu.roll(mid, 1, 1) + pltpu.roll(mid, 15, 1)
            near = near + turn(mid, 4) * low_ok[4][0, :, 0:1] + turn(mid, -4) * high_ok[4][0, :, 0:1]
            est = 0.3 * mid + far_inv[lo:hi] * (b[lo:hi] + 4.0 * near)
        far_est[...] = est
        b1 = one_rhs[...]
        inv1 = one_inv[...]
        e2 = jnp.stack(
            [
                jnp.stack(
                    [
                        jnp.take_along_axis(
                            jnp.broadcast_to(far_est[x, 3 + y : 4 + y, :], (8, LANES)),
                            unpack_index,
                            axis=1,
                            mode="promise_in_bounds",
                        )[0:3]
                        for y in range(3)
                    ]
                )
                for x in range(3)
            ]
        )
        e1 = inv1 * b1 + finer(e2)
        mid = e1[1:5, 1:5]
        near = e1[0:4, 1:5] + e1[2:6, 1:5] + e1[1:5, 0:4] + e1[1:5, 2:6] + beside_z(mid, 2)
        e1 = 0.3 * mid + inv1[1:5, 1:5] * (b1[1:5, 1:5] + 2.0 * near)
        e0 = e0_ref[1:9, 1:9] + finer(e1)
        mid = e0[1:7, 1:7]
        near = e0[0:6, 1:7] + e0[2:8, 1:7] + e0[1:7, 0:6] + e0[1:7, 2:8] + beside_z(mid, 1)
        field[...] = 0.3 * mid + inv0[2:8, 2:8] * (rhs[2:8, 2:8] + near)

    def down(v):
        return jnp.sum(v.sum(axis=(0, 1)), axis=0, keepdims=True)

    def early_sums():
        sums[...] = jnp.zeros_like(sums)
        sums[0:1] = down(rhs0[3:7, 3:7] * z_ref[1:5, 1:5])
        sums[1:2] = down(rhs1[3:7, 3:7] * z_ref[1:5, 1:5])

    for i, d in enumerate(NEAR):
        got = first_in[i]
        arrived(got, 0, i)
        sx, sy = box(first_place, d)
        rhs0[sx, sy] = got[:, :, 0:3, :]
        mass[sx, sy] = got[:, :, 3:4, :]
    for x in range(10):
        for y in range(10):
            mass_rows[x, y : y + 1, :] = mass[x, y]
    at_x = lax.broadcasted_iota(jnp.int32, (10, 16, LANES), 0) + (gx * 4 - 3)
    at_y = lax.broadcasted_iota(jnp.int32, (10, 16, LANES), 1) + (gy * 4 - 3)
    within = (at_x >= 0) & (at_x < 4 * n_gx) & (at_y >= 0) & (at_y < 4 * n_gy)
    inv_rows[...] = jnp.where(within, 0.7 / (mass_rows[...] + 6.0), 0.0)
    for x in range(10):
        for y in range(10):
            inv0[x, y] = jnp.broadcast_to(inv_rows[x, y : y + 1, :], (3, LANES))
    first_half()
    second_half(0, rhs0, z_ref)
    for x in (1, 8):
        e0_ref[x : x + 1, 1:9] = jnp.zeros((1, 8, 3, LANES), F32)
        e0_ref[1:9, x : x + 1] = jnp.zeros((8, 1, 3, LANES), F32)
    stress, _ = strains(z_ref)
    forces(stress, z_ref, part0)

    def kept(d):
        keep = jnp.bool_(True)
        if d[0]:
            keep = keep & ((gx > 0) if d[0] < 0 else (gx < n_gx - 1))
        if d[1]:
            keep = keep & ((gy > 0) if d[1] < 0 else (gy < n_gy - 1))
        return jnp.where(keep, 1.0, 0.0).astype(F32)

    own_share()
    for i, d in DIAGONAL_FIRST:
        send(few_out.at[3 * d[0] + d[1] + 4], few_in.at[other(d)], 5, i, d)
    for i, d in enumerate(NEAR):
        if d[0] and d[1]:
            n = (2, 3, 4, 5).index(i)
            for k, (p, q) in enumerate(CORNER):
                corner_out[n, k] = part0[5 - p if d[0] > 0 else p, 5 - q if d[1] > 0 else q]
            send(corner_out.at[n], wide_in[other(d)], 3, i, d)
        else:
            sx, sy = box(wide_cut, d)
            send(part0.at[sx, sy], wide_in[other(d)], 3, i, d)
    rhs1[2:8, 2:8] = part0[...]
    coarse = few_out[4]
    for i, d in enumerate(NEAR):
        arrived(few_in.at[i], 5, i)
        coarse = coarse + few_in[i] * kept(d)
    far_own1[...] = coarse
    far_start(1)
    for i, d in enumerate(NEAR):
        got = wide_in[i]
        arrived(got, 3, i)
        if d[0] and d[1]:
            for k, (p, q) in enumerate(CORNER):
                x, y = (3 - p if d[0] < 0 else 6 + p), (3 - q if d[1] < 0 else 6 + q)
                rhs1[x, y] = rhs1[x, y] + got[k] * kept(d)
        else:
            sx, sy = box(wide_place, d)
            rhs1[sx, sy] = rhs1[sx, sy] + got[...] * kept(d)
    e0_ref[1:9, 1:9] = inv0[1:9, 1:9] * rhs1[1:9, 1:9]
    r0 = (
        0.3 * rhs1[3:7, 3:7]
        + e0_ref[2:6, 3:7]
        + e0_ref[4:8, 3:7]
        + e0_ref[3:7, 2:6]
        + e0_ref[3:7, 4:8]
        + beside_z(e0_ref[3:7, 3:7], 1)
    )
    one_own1[...] = coarser(r0, 1)
    one_start(1)
    early_sums()
    second_half(1, rhs1, u_ref)
    stress, energy = strains(u_ref)

    def line_start(src, slots, stage, count, step):
        for d in range(1, count):
            copy = pltpu.make_async_remote_copy(
                src_ref=src,
                dst_ref=slots.at[d - 1],
                send_sem=line_send.at[stage],
                recv_sem=line_recv.at[stage],
                device_id=device(*step(d)),
                device_id_type=MESH,
            )
            copy.start()
        closers.append((slots.at[pl.ds(0, count - 1)], line_send.at[stage]))

    def line_end(src, slots, stage, count):
        whole = slots.at[pl.ds(0, count - 1)]
        pltpu.make_async_copy(whole, whole, line_recv.at[stage]).wait()
        total = src[...]
        for d in range(1, count):
            total = total + slots[d - 1]
        return total

    b = rhs0[3:7, 3:7]
    w = rhs1[3:7, 3:7]
    z = z_ref[1:5, 1:5]
    u = u_ref[1:5, 1:5]
    own_mass = jnp.broadcast_to(mass[3:7, 3:7], z.shape)
    sums[2:3] = down(b * u)
    sums[3:4] = down(w * u)
    sums[4:5] = down(own_mass * u * u) + jnp.sum(energy, axis=0, keepdims=True)
    across = jnp.broadcast_to(jnp.sum(sums[...], axis=1, keepdims=True), (8, LANES))
    sum_own[...] = jnp.sum(jnp.where(lane2 == sub2, across, 0.0), axis=0, keepdims=True)
    line_start(sum_own, line_in, 0, n_gx, lambda d: (farthest(n_gx)[d - 1], 0))
    forces(stress, u_ref, part1)
    for i, d in enumerate(NEAR):
        sx, sy = box(thin_cut, d)
        send(part1.at[sx, sy], thin_in[other(d)], 4, i, d)
    sum_own2[...] = line_end(sum_own, line_in, 0, n_gx)
    line_start(sum_own2, line_in2, 1, n_gy, lambda d: (0, farthest(n_gy)[d - 1]))
    total = line_end(sum_own2, line_in2, 1, n_gy)

    def scalar(i):
        index = jnp.full((8, LANES), i, jnp.int32)
        return jnp.take_along_axis(
            jnp.broadcast_to(total, (8, LANES)), index, axis=1, mode="promise_in_bounds"
        )

    bz, zw, bu, wu, uv = (scalar(i) for i in range(5))
    step0 = bz / zw
    rz1 = bz - step0 * (bu + zw) + step0 * step0 * wu
    ratio = rz1 / bz
    mixed = zw - step0 * wu
    curve = zw - 2.0 * step0 * wu + step0 * step0 * uv + 2.0 * ratio * mixed + ratio * ratio * zw
    step1 = rz1 / curve
    first = (step0 + step1 + step1 * ratio)[0:3]
    second = (step1 * step0)[0:3]

    answer[...] = first * z - second * u
    for n in range(48):
        x, y, m = n // 12, n // 3 % 4, n % 3
        x_ref[m, x, y : y + 1, :] = answer[x, y, m : m + 1, :]
    e0_ref[0:4, 0:4] = part1[1:5, 1:5]
    for i, d in enumerate(NEAR):
        arrived(thin_in[i], 4, i)
        sx, sy = box(thin_place, d)
        e0_ref[sx, sy] = e0_ref[sx, sy] + thin_in[i][...] * kept(d)
    answer[...] = b - first * w + second * e0_ref[0:4, 0:4]
    for n in range(48):
        x, y, m = n // 12, n // 3 % 4, n % 3
        r_ref[m, x, y : y + 1, :] = answer[x, y, m : m + 1, :]
    close()


def solution(mesh):
    n_gx, n_gy = mesh.shape["gx"], mesh.shape["gy"]

    def vmem(*shape, dtype=F32):
        return pltpu.VMEM(shape, dtype)

    scratch = [vmem(*extent(first_cut, (-d[0], -d[1]), 4)) for d in NEAR]
    scratch += [
        vmem(len(CORNER), 3, LANES) if d[0] and d[1] else vmem(*extent(wide_cut, (-d[0], -d[1]), 3))
        for d in NEAR
    ]
    scratch += [vmem(*extent(thin_cut, (-d[0], -d[1]), 3)) for d in NEAR]
    scratch += [vmem(2, 2, 4, LANES) for _ in range(8)]
    scratch += [vmem(2, 2, 3, LANES) for _ in range(8)]
    scratch += [
        vmem(3, 4, 4, LANES), vmem(4, 4, LANES),
        vmem(8, LANES), vmem(8, LANES, dtype=jnp.int32), vmem(8, LANES, dtype=jnp.int32),
    ]
    scratch += [
        vmem(81, 8, LANES),
        vmem(4, 4, 4, LANES),
        vmem(10, 10, 3, LANES),
        vmem(10, 10, 3, LANES),
        vmem(10, 10, 1, LANES),
        vmem(10, 10, 3, LANES),
        vmem(10, 10, 3, LANES),
        vmem(2, 2, 4, LANES),
        vmem(2, 2, 3, LANES),
        vmem(6, 6, 3, LANES),
        vmem(6, 6, 3, LANES),
        vmem(1, LANES),
        vmem(1, LANES),
        vmem(81, 1, LANES),
        vmem(81, 1, LANES),
        vmem(9, 16, LANES),
        vmem(9, 16, LANES),
        vmem(3, 16, LANES),
        vmem(6, 6, 3, LANES),
        vmem(6, 6, 3, LANES),
        vmem(3, 6, 6, 3, LANES),
        vmem(3 * ROWS * 8, LANES),
        vmem(LANES, 8 * LANES, dtype=BF16),
        vmem(ROWS, LANES),
        vmem(6, 6, 3, LANES),
        vmem(6, 6, 3, LANES),
        vmem(8, LANES),
        vmem(1, LANES),
        vmem(1, LANES),
        vmem(n_gx, 1, LANES),
        vmem(n_gy, 1, LANES),
        vmem(4, 4, 3, LANES),
        vmem(4, len(CORNER), 3, LANES),
        vmem(9, 1, LANES),
        vmem(8, 1, LANES),
        vmem(6, 6, 3, LANES),
        vmem(8, 8, 3, LANES),
        vmem(6, 6, 3, LANES),
        vmem(10, 16, LANES),
        vmem(10, 16, LANES),
        pltpu.SemaphoreType.DMA((6, 8)),
        pltpu.SemaphoreType.DMA((6, 8)),
        pltpu.SemaphoreType.DMA((2,)),
        pltpu.SemaphoreType.DMA((2,)),
        pltpu.SemaphoreType.DMA((2,)),
        pltpu.SemaphoreType.DMA((2,)),
        pltpu.SemaphoreType.DMA((6,)),
    ]

    def body(right, mass, gradients, *rest):
        by_tile = jnp.transpose(gradients[0, 0], (1, 2, 0, 3)).reshape(81, 8, LANES)
        args = (right, mass, by_tile) + rest
        call = pl.pallas_call(
            lambda *refs: kernel(n_gx, n_gy, *refs),
            out_shape=pltpu.VMEM((2, 3, 4, 4, LANES), F32),
            in_specs=[pl.BlockSpec(memory_space=pl.ANY)] * 6,
            out_specs=pl.BlockSpec(memory_space=pltpu.VMEM),
            scratch_shapes=scratch,
            compiler_params=pltpu.CompilerParams(collective_id=0, has_side_effects=True),
            name="cg",
        )
        both = call(*args)
        return both[0], both[1]

    field = P(None, "gx", "gy", None)
    block = P("gx", "gy", None, None)
    return jax.shard_map(
        body,
        mesh=mesh,
        in_specs=(field, P("gx", "gy", None), P("gx", "gy", None, None, None, None)) + (block,) * 3,
        out_specs=(field, field),
        check_vma=False,
    )
```

```python
import jax
import jax.numpy as jnp
from jax import lax
from jax.experimental import pallas as pl
from jax.experimental.pallas import tpu as pltpu
from jax.sharding import PartitionSpec as P

MESH = pl.DeviceIdType.MESH
F32 = jnp.float32
BF16 = jnp.bfloat16
LANES = 128
POISSON = 0.3
NEAR = tuple(
    (dx, dy)
    for dx, dy in ((0, 1), (0, -1), (1, 1), (1, -1), (-1, 1), (-1, -1), (1, 0), (-1, 0))
)
DIAGONAL_FIRST = tuple(sorted(enumerate(NEAR), key=lambda e: -abs(e[1][0]) - abs(e[1][1])))
FAR = tuple(
    sorted(
        (
            (dx, dy)
            for dx in range(-4, 5)
            for dy in range(-4, 5)
            if (dx, dy) != (0, 0) and max(abs(dx) - 1, 0) + max(abs(dy) - 1, 0) <= 3
        ),
        key=lambda d: (-abs(d[1]) - (0, 2, 2, 3, 3)[abs(d[0])], -abs(d[1])),
    )
)
GREETED = tuple(
    (dx, dy)
    for dx in range(-3, 4)
    for dy in range(-3, 4)
    if 0 < abs(dx) + abs(dy) <= 3
) + tuple((d, 0) for d in (14, 15, 16, -15, -14))
CORNER = tuple((p, q) for p in range(3) for q in range(3) if p + q <= 3)
ROWS = 112


def farthest(n):
    return sorted(range(1, n), key=lambda d: (-min(d, n - d), d))


def first_cut(d, diagonal):
    if d == 0:
        return (0, 4)
    wide = 2 if diagonal else 3
    return (4 - wide, 4) if d > 0 else (0, wide)


def first_place(d, diagonal):
    if d == 0:
        return (3, 7)
    wide = 2 if diagonal else 3
    return (7, 7 + wide) if d > 0 else (3 - wide, 3)


def wide_cut(d, diagonal):
    return ((0, 3), (0, 6), (3, 6))[d + 1]


def wide_place(d, diagonal):
    return ((1, 4), (2, 8), (6, 9))[d + 1]


def thin_cut(d, diagonal):
    return ((0, 1), (1, 5), (5, 6))[d + 1]


def thin_place(d, diagonal):
    return ((0, 1), (0, 4), (3, 4))[d + 1]


def box(cut, d):
    diagonal = d[0] != 0 and d[1] != 0
    (x0, x1), (y0, y1) = cut(d[0], diagonal), cut(d[1], diagonal)
    return slice(x0, x1), slice(y0, y1)


def extent(cut, d, rows):
    sx, sy = box(cut, d)
    return (sx.stop - sx.start, sy.stop - sy.start, rows, LANES)


def kernel(n_gx, n_gy, *refs):
    (b_hbm, m_hbm, g_hbm, s_hbm, v_hbm, n_hbm, both_ref), refs = refs[:7], refs[7:]
    x_ref, r_ref = both_ref.at[0], both_ref.at[1]
    first_in, wide_in, thin_in = refs[:8], refs[8:16], refs[16:24]
    one_in = (refs[24:32], refs[32:40])
    (b_in, m_in, s_in, v_in, n_in), refs = refs[40:45], refs[45:]
    (
        grad, own, rhs0, rhs1, mass, inv0, e0_ref, one_own0, one_own1, one_rhs, one_inv,
        far_own0, far_own1, far_in0, far_in1, far_inv, far_est, z_ref, u_ref,
        z_shift, f_rows, hot, rows_out, part0, part1, sums, sum_own,
        sum_own2, line_in, line_in2, answer, corner_out, few_out, few_in, one_pad, fine_pad, one_share, mass_rows, inv_rows, near_send, near_recv, far_send, far_recv,
        line_send, line_recv, local_sem,
    ) = refs

    gx, gy = lax.axis_index("gx"), lax.axis_index("gy")

    def device(dx, dy):
        return {"gx": lax.rem(gx + (dx % n_gx), n_gx), "gy": lax.rem(gy + (dy % n_gy), n_gy)}

    loads = [
        pltpu.make_async_copy(src, dst, local_sem.at[i])
        for i, (src, dst) in enumerate(
            (
                (b_hbm, b_in), (m_hbm, m_in), (g_hbm, grad),
                (s_hbm.at[0, 0], s_in), (v_hbm.at[0, 0], v_in), (n_hbm.at[0, 0], n_in),
            )
        )
    ]
    for load in loads:
        load.start()
    partners = list(NEAR) + sorted(set(GREETED) - set(NEAR))
    barrier = pltpu.get_barrier_semaphore()
    for dx, dy in partners:
        pl.semaphore_signal(barrier, inc=1, device_id=device(dx, dy), device_id_type=MESH)
    for load in (loads[0], loads[1]):
        load.wait()
    for x in range(4):
        for y in range(4):
            for m in range(3):
                own[x, y, m : m + 1, :] = b_in[m, x, y : y + 1, :]
            own[x, y, 3:4, :] = m_in[x, y : y + 1, :]
    rhs0[3:7, 3:7] = own[:, :, 0:3, :]
    mass[3:7, 3:7] = own[:, :, 3:4, :]

    pl.semaphore_wait(barrier, len(partners))

    started = []
    closers = []

    def close():
        for copy in started:
            copy.wait_send()
        for whole, sem in closers:
            pltpu.make_async_copy(whole, whole, sem).wait()

    def send(src, dst, group, i, d):
        copy = pltpu.make_async_remote_copy(
            src_ref=src,
            dst_ref=dst,
            send_sem=near_send.at[group, i],
            recv_sem=near_recv.at[group, NEAR.index((-d[0], -d[1]))],
            device_id=device(*d),
            device_id_type=MESH,
        )
        copy.start()
        started.append(copy)

    def arrived(dst, group, i):
        pltpu.make_async_copy(dst, dst, near_recv.at[group, i]).wait()

    def other(d):
        return NEAR.index((-d[0], -d[1]))

    for i, d in DIAGONAL_FIRST:
        sx, sy = box(first_cut, d)
        send(own.at[sx, sy], first_in[other(d)], 0, i, d)

    lane4 = lax.broadcasted_iota(jnp.int32, (1, 1, 3, LANES), 3)

    def ones_where(cond):
        return jnp.where(cond, 1.0, 0.0).astype(F32)

    low_ok = {s: ones_where(lane4 >= s) for s in (1, 2, 4)}
    high_ok = {s: ones_where(lane4 < LANES - s) for s in (1, 2, 4)}
    odd = {s: ones_where((lane4 & s) != 0) for s in (1, 2)}
    even = {s: ones_where((lane4 & s) == 0) for s in (1, 2)}

    def turn(v, s):
        return pltpu.roll(v, s % LANES, v.ndim - 1)

    def beside_z(v, s):
        return turn(v, s) * low_ok[s] + turn(v, -s) * high_ok[s]

    def pair_z(v, s):
        return v + turn(v, s) * odd[s] + turn(v, -s) * even[s]

    def coarser(v, s):
        nx, ny = v.shape[0] // 2, v.shape[1] // 2
        w = v.reshape((nx, 2, ny, 2) + v.shape[2:])
        w = (w[:, 0] + w[:, 1])
        w = w[:, :, 0] + w[:, :, 1]
        return pair_z(w, s)

    def finer(v):
        nx, ny = v.shape[:2]
        w = jnp.broadcast_to(v[:, None, :, None], (nx, 2, ny, 2) + v.shape[2:])
        return w.reshape((2 * nx, 2 * ny) + v.shape[2:])

    lane2 = lax.broadcasted_iota(jnp.int32, (8, LANES), 1)
    sub2 = lax.broadcasted_iota(jnp.int32, (8, LANES), 0)
    pack_mask = ones_where((lane2 & 3) == sub2)[0:3]
    mass_mask = ones_where((lane2 & 3) == 3)[0:1]
    unpack_index = (lane2 & ~3) + jnp.minimum(sub2, 2)
    inside = (
        (ones_where(gx > 0), ones_where(gx < n_gx - 1)),
        (ones_where(gy > 0), ones_where(gy < n_gy - 1)),
    )

    for load in loads[2:]:
        load.wait()
    node = n_in[...]
    quotient = (node * 2017) >> 18
    k_index = node - quotient * 130
    i_index = (quotient * 43) >> 8
    j_index = quotient - i_index * 6
    effective = s_in[...] * v_in[...].astype(F32)
    z_rows = lax.broadcasted_iota(jnp.int32, (LANES, LANES), 0)
    for s in range(8):
        same = jnp.broadcast_to(k_index[s : s + 1, :], (LANES, LANES)) == z_rows
        hot[:, s * LANES : (s + 1) * LANES] = ones_where(same).astype(BF16)
    shear = effective * (0.5 / (1.0 + POISSON))
    lame = effective * (POISSON / ((1.0 + POISSON) * (1.0 - 2.0 * POISSON)))

    def strains(field):
        v = field[...]
        z_shift[0] = turn(v, 1) * low_ok[1]
        z_shift[1] = v
        z_shift[2] = turn(v, -1) * high_ok[1]
        i_lo, i_hi = (i_index & 1) != 0, (i_index & 2) != 0
        j_lo, j_hi = (j_index & 1) != 0, (j_index & 2) != 0

        def four(v0, v1, v2, v3, lo, hi):
            return jnp.where(hi, jnp.where(lo, v3, v2), jnp.where(lo, v1, v0))

        def gather(c, disp):
            disp = list(disp)
            for m in range(3):
                picked = [
                    [
                        jnp.take_along_axis(
                            jnp.broadcast_to(z_shift[c, x, y, m : m + 1, :], (8, LANES)),
                            k_index,
                            axis=1,
                            mode="promise_in_bounds",
                        )
                        for y in range(6)
                    ]
                    for x in range(6)
                ]
                for a in range(3):
                    row = [
                        four(*(picked[a + i][y] for i in range(4)), i_lo, i_hi) for y in range(6)
                    ]
                    for b in range(3):
                        value = four(*row[b : b + 4], j_lo, j_hi)
                        for l in range(3):
                            at = grad[l * 27 + 9 * a + 3 * b + c]
                            disp[3 * m + l] = disp[3 * m + l] + value * at
            return tuple(disp)

        zero = jnp.zeros((8, LANES), F32)
        disp = lax.fori_loop(0, 3, gather, (zero,) * 9)
        trace = lame * (disp[0] + disp[4] + disp[8])
        stress = [
            shear * (disp[3 * m + l] + disp[3 * l + m]) + (trace if m == l else 0.0)
            for m in range(3)
            for l in range(3)
        ]
        return stress, sum(stress[q] * disp[q] for q in range(9))

    def forces(stress, field, part):
        def scatter(c, carry):
            for m in range(3):
                spread = []
                for a in range(3):
                    force = []
                    for b in range(3):
                        t = 9 * a + 3 * b + c
                        force.append(sum(stress[3 * m + l] * grad[l * 27 + t] for l in range(3)))
                    spread.append(
                        [
                            sum(
                                jnp.where(j_index == y - b, force[b], 0.0)
                                for b in range(3)
                                if 0 <= y - b <= 3
                            )
                            for y in range(6)
                        ]
                    )
                for x in range(6):
                    for y in range(6):
                        row = pl.multiple_of((c * ROWS + (x * 6 + y) * 3 + m) * 8, 8)
                        f_rows[pl.ds(row, 8), :] = sum(
                            jnp.where(i_index == x - a, spread[a][y], 0.0)
                            for a in range(3)
                            if 0 <= x - a <= 3
                        )
            return carry

        lax.fori_loop(0, 3, scatter, 0)
        contract = (((1,), (1,)), ((), ()))
        total = None
        for pair in range(4):
            rows = jnp.concatenate(
                [f_rows[pl.ds(2 * pair + q, 3 * ROWS, stride=8), :] for q in range(2)], axis=1
            )
            mine = hot[:, 2 * pair * LANES : (2 * pair + 2) * LANES]
            high = rows.astype(BF16)
            low = (rows - high.astype(F32)).astype(BF16)
            for value in (high, low):
                term = lax.dot_general(value, mine, contract, preferred_element_type=F32)
                total = term if total is None else total + term
        rows_out[...] = (
            turn(total[0:ROWS], -1) * high_ok[1][0, 0, 0:1]
            + total[ROWS : 2 * ROWS]
            + turn(total[2 * ROWS : 3 * ROWS], 1) * low_ok[1][0, 0, 0:1]
        )
        for n in range(36):
            part[n // 6, n % 6] = rows_out[3 * n : 3 * n + 3, :]
        part[1:5, 1:5] = part[1:5, 1:5] + mass[3:7, 3:7] * field[1:5, 1:5]

    def fine_residual(rhs):
        e0_ref[...] = inv0[...] * rhs[...]
        return (
            0.3 * rhs[1:9, 1:9]
            + e0_ref[0:8, 1:9]
            + e0_ref[2:10, 1:9]
            + e0_ref[1:9, 0:8]
            + e0_ref[1:9, 2:10]
            + beside_z(e0_ref[1:9, 1:9], 1)
        )

    def far_start(turn_no):
        far_own = (far_own0, far_own1)[turn_no]
        far_slots = (far_in0, far_in1)[turn_no]
        for dx, dy in FAR:
            copy = pltpu.make_async_remote_copy(
                src_ref=far_own,
                dst_ref=far_slots.at[4 - dx, pl.ds(4 - dy, 1), :],
                send_sem=far_send.at[turn_no],
                recv_sem=far_recv.at[turn_no],
                device_id=device(dx, dy),
                device_id_type=MESH,
            )
            copy.start()

    def one_start(turn_no):
        for i, d in enumerate(NEAR):
            one_own = (one_own0, one_own1)[turn_no]
            send(one_own, one_in[turn_no][other(d)], 1 + turn_no, i, d)

    def first_half():
        b1 = coarser(fine_residual(rhs0), 1)
        mass1 = coarser(jnp.broadcast_to(mass[1:9, 1:9], (8, 8, 3, LANES)), 1)
        inv1 = 0.7 / (mass1 + 12.0)
        one_inv[1:5, 1:5] = inv1
        one_inv[1:2, 1:5] = one_inv[1:2, 1:5] * inside[0][0]
        one_inv[4:5, 1:5] = one_inv[4:5, 1:5] * inside[0][1]
        one_inv[1:5, 1:2] = one_inv[1:5, 1:2] * inside[1][0]
        one_inv[1:5, 4:5] = one_inv[1:5, 4:5] * inside[1][1]
        e1 = one_inv[1:5, 1:5] * b1
        r1 = 0.3 * b1[1:3, 1:3] + 2.0 * (
            e1[0:2, 1:3] + e1[2:4, 1:3] + e1[1:3, 0:2] + e1[1:3, 2:4] + beside_z(e1[1:3, 1:3], 2)
        )
        b2 = coarser(r1, 2)[0, 0]
        mass2 = coarser(mass1[1:3, 1:3], 2)[0, 0]
        far_own0[...] = (
            jnp.sum(b2 * pack_mask, axis=0, keepdims=True) + mass2[0:1] * mass_mask
        )
        far_start(0)
        one_own0[:, :, 0:3, :] = b1[1:3, 1:3]
        one_own0[:, :, 3:4, :] = mass1[1:3, 1:3, 0:1]
        one_start(0)
        for pad in (fine_pad, one_pad, one_share, rhs1):
            pad[...] = jnp.zeros_like(pad)

    def own_share():
        est = inv0[2:8, 2:8] * part0[...]
        e0_ref[2:8, 2:8] = est
        fine_pad[1:7, 1:7] = (
            0.3 * part0[...]
            + e0_ref[1:7, 2:8]
            + e0_ref[3:9, 2:8]
            + e0_ref[2:8, 1:7]
            + e0_ref[2:8, 3:9]
            + beside_z(est, 1)
        )
        fine_pad[0:1, 1:7] = est[0:1]
        fine_pad[7:8, 1:7] = est[5:6]
        fine_pad[1:7, 0:1] = est[:, 0:1]
        fine_pad[1:7, 7:8] = est[:, 5:6]
        b1 = coarser(fine_pad[...], 1)
        est = one_inv[1:5, 1:5] * b1
        one_pad[1:5, 1:5] = est
        one_share[1:5, 1:5] = 0.3 * b1 + 2.0 * (
            one_pad[0:4, 1:5]
            + one_pad[2:6, 1:5]
            + one_pad[1:5, 0:4]
            + one_pad[1:5, 2:6]
            + beside_z(est, 2)
        )
        one_share[0:1, 1:5] = 2.0 * est[0:1]
        one_share[5:6, 1:5] = 2.0 * est[3:4]
        one_share[1:5, 0:1] = 2.0 * est[:, 0:1]
        one_share[1:5, 5:6] = 2.0 * est[:, 3:4]
        r1 = one_share[...]
        b2 = coarser(r1, 2)
        for x in range(3):
            for y in range(3):
                few_out[3 * x + y] = jnp.sum(b2[x, y] * pack_mask, axis=0, keepdims=True)

    def second_half(turn_no, rhs, field):
        far_own = (far_own0, far_own1)[turn_no]
        far_slots = (far_in0, far_in1)[turn_no]
        one_own = (one_own0, one_own1)[turn_no]
        one_rhs[2:4, 2:4] = one_own[:, :, 0:3, :]
        for i, d in enumerate(NEAR):
            got = one_in[turn_no][i]
            arrived(got, 1 + turn_no, i)
            sx, sy = slice(2 + 2 * d[0], 4 + 2 * d[0]), slice(2 + 2 * d[1], 4 + 2 * d[1])
            one_rhs[sx, sy] = got[:, :, 0:3, :]
            if turn_no == 0:
                keep = jnp.float32(1.0)
                if d[0]:
                    keep = keep * inside[0][(d[0] + 1) // 2]
                if d[1]:
                    keep = keep * inside[1][(d[1] + 1) // 2]
                beside = jnp.broadcast_to(got[:, :, 3:4, :], (2, 2, 3, LANES))
                one_inv[sx, sy] = (0.7 / (beside + 12.0)) * keep
        far_all = far_slots.at[pl.ds(0, 7), pl.ds(0, 8), :]
        closers.append((far_all, far_send.at[turn_no]))
        pltpu.make_async_copy(far_all, far_all, far_recv.at[turn_no]).wait()
        far_slots[4, 4:5, :] = far_own[...]
        b = far_slots[...]
        if turn_no == 0:
            quarter = lax.broadcasted_iota(jnp.int32, b.shape, 2) & 3
            diagonal = jnp.where(
                quarter == 0, turn(b, -3), jnp.where(quarter == 1, turn(b, -2), turn(b, -1))
            )
            at_x = lax.broadcasted_iota(jnp.int32, b.shape, 0) + (gx - 4)
            at_y = lax.broadcasted_iota(jnp.int32, b.shape, 1) + (gy - 4)
            within = (at_x >= 0) & (at_x < n_gx) & (at_y >= 0) & (at_y < n_gy)
            far_inv[...] = jnp.where(within, 0.7 / (diagonal + 24.0), 0.0)
        est = far_inv[...] * b
        for sweep in range(3):
            lo, hi = sweep + 1, 8 - sweep
            mid = est[1:-1]
            near = est[:-2] + est[2:] + pltpu.roll(mid, 1, 1) + pltpu.roll(mid, 15, 1)
            near = near + turn(mid, 4) * low_ok[4][0, :, 0:1] + turn(mid, -4) * high_ok[4][0, :, 0:1]
            est = 0.3 * mid + far_inv[lo:hi] * (b[lo:hi] + 4.0 * near)
        far_est[...] = est
        b1 = one_rhs[...]
        inv1 = one_inv[...]
        e2 = jnp.stack(
            [
                jnp.stack(
                    [
                        jnp.take_along_axis(
                            jnp.broadcast_to(far_est[x, 3 + y : 4 + y, :], (8, LANES)),
                            unpack_index,
                            axis=1,
                            mode="promise_in_bounds",
                        )[0:3]
                        for y in range(3)
                    ]
                )
                for x in range(3)
            ]
        )
        e1 = inv1 * b1 + finer(e2)
        mid = e1[1:5, 1:5]
        near = e1[0:4, 1:5] + e1[2:6, 1:5] + e1[1:5, 0:4] + e1[1:5, 2:6] + beside_z(mid, 2)
        e1 = 0.3 * mid + inv1[1:5, 1:5] * (b1[1:5, 1:5] + 2.0 * near)
        e0 = e0_ref[1:9, 1:9] + finer(e1)
        mid = e0[1:7, 1:7]
        near = e0[0:6, 1:7] + e0[2:8, 1:7] + e0[1:7, 0:6] + e0[1:7, 2:8] + beside_z(mid, 1)
        field[...] = 0.3 * mid + inv0[2:8, 2:8] * (rhs[2:8, 2:8] + near)

    def down(v):
        return jnp.sum(v.sum(axis=(0, 1)), axis=0, keepdims=True)

    def early_sums():
        sums[...] = jnp.zeros_like(sums)
        sums[0:1] = down(rhs0[3:7, 3:7] * z_ref[1:5, 1:5])
        sums[1:2] = down(rhs1[3:7, 3:7] * z_ref[1:5, 1:5])

    for i, d in enumerate(NEAR):
        got = first_in[i]
        arrived(got, 0, i)
        sx, sy = box(first_place, d)
        rhs0[sx, sy] = got[:, :, 0:3, :]
        mass[sx, sy] = got[:, :, 3:4, :]
    for x in range(10):
        for y in range(10):
            mass_rows[x, y : y + 1, :] = mass[x, y]
    at_x = lax.broadcasted_iota(jnp.int32, (10, 16, LANES), 0) + (gx * 4 - 3)
    at_y = lax.broadcasted_iota(jnp.int32, (10, 16, LANES), 1) + (gy * 4 - 3)
    within = (at_x >= 0) & (at_x < 4 * n_gx) & (at_y >= 0) & (at_y < 4 * n_gy)
    inv_rows[...] = jnp.where(within, 0.7 / (mass_rows[...] + 6.0), 0.0)
    for x in range(10):
        for y in range(10):
            inv0[x, y] = jnp.broadcast_to(inv_rows[x, y : y + 1, :], (3, LANES))
    first_half()
    second_half(0, rhs0, z_ref)
    for x in (1, 8):
        e0_ref[x : x + 1, 1:9] = jnp.zeros((1, 8, 3, LANES), F32)
        e0_ref[1:9, x : x + 1] = jnp.zeros((8, 1, 3, LANES), F32)
    stress, _ = strains(z_ref)
    forces(stress, z_ref, part0)

    def kept(d):
        keep = jnp.bool_(True)
        if d[0]:
            keep = keep & ((gx > 0) if d[0] < 0 else (gx < n_gx - 1))
        if d[1]:
            keep = keep & ((gy > 0) if d[1] < 0 else (gy < n_gy - 1))
        return jnp.where(keep, 1.0, 0.0).astype(F32)

    own_share()
    for i, d in DIAGONAL_FIRST:
        send(few_out.at[3 * d[0] + d[1] + 4], few_in.at[other(d)], 5, i, d)
    for i, d in enumerate(NEAR):
        if d[0] and d[1]:
            n = (2, 3, 4, 5).index(i)
            for k, (p, q) in enumerate(CORNER):
                corner_out[n, k] = part0[5 - p if d[0] > 0 else p, 5 - q if d[1] > 0 else q]
            send(corner_out.at[n], wide_in[other(d)], 3, i, d)
        else:
            sx, sy = box(wide_cut, d)
            send(part0.at[sx, sy], wide_in[other(d)], 3, i, d)
    rhs1[2:8, 2:8] = part0[...]
    coarse = few_out[4]
    for i, d in enumerate(NEAR):
        arrived(few_in.at[i], 5, i)
        coarse = coarse + few_in[i] * kept(d)
    far_own1[...] = coarse
    far_start(1)
    for i, d in enumerate(NEAR):
        got = wide_in[i]
        arrived(got, 3, i)
        if d[0] and d[1]:
            for k, (p, q) in enumerate(CORNER):
                x, y = (3 - p if d[0] < 0 else 6 + p), (3 - q if d[1] < 0 else 6 + q)
                rhs1[x, y] = rhs1[x, y] + got[k] * kept(d)
        else:
            sx, sy = box(wide_place, d)
            rhs1[sx, sy] = rhs1[sx, sy] + got[...] * kept(d)
    e0_ref[1:9, 1:9] = inv0[1:9, 1:9] * rhs1[1:9, 1:9]
    r0 = (
        0.3 * rhs1[3:7, 3:7]
        + e0_ref[2:6, 3:7]
        + e0_ref[4:8, 3:7]
        + e0_ref[3:7, 2:6]
        + e0_ref[3:7, 4:8]
        + beside_z(e0_ref[3:7, 3:7], 1)
    )
    one_own1[...] = coarser(r0, 1)
    one_start(1)
    early_sums()
    second_half(1, rhs1, u_ref)
    stress, energy = strains(u_ref)

    def line_start(src, slots, stage, count, step):
        for d in range(1, count):
            copy = pltpu.make_async_remote_copy(
                src_ref=src,
                dst_ref=slots.at[d - 1],
                send_sem=line_send.at[stage],
                recv_sem=line_recv.at[stage],
                device_id=device(*step(d)),
                device_id_type=MESH,
            )
            copy.start()
        closers.append((slots.at[pl.ds(0, count - 1)], line_send.at[stage]))

    def line_end(src, slots, stage, count):
        whole = slots.at[pl.ds(0, count - 1)]
        pltpu.make_async_copy(whole, whole, line_recv.at[stage]).wait()
        total = src[...]
        for d in range(1, count):
            total = total + slots[d - 1]
        return total

    b = rhs0[3:7, 3:7]
    w = rhs1[3:7, 3:7]
    z = z_ref[1:5, 1:5]
    u = u_ref[1:5, 1:5]
    own_mass = jnp.broadcast_to(mass[3:7, 3:7], z.shape)
    sums[2:3] = down(b * u)
    sums[3:4] = down(w * u)
    sums[4:5] = down(own_mass * u * u) + jnp.sum(energy, axis=0, keepdims=True)
    across = jnp.broadcast_to(jnp.sum(sums[...], axis=1, keepdims=True), (8, LANES))
    sum_own[...] = jnp.sum(jnp.where(lane2 == sub2, across, 0.0), axis=0, keepdims=True)
    line_start(sum_own, line_in, 0, n_gx, lambda d: (farthest(n_gx)[d - 1], 0))
    forces(stress, u_ref, part1)
    for i, d in enumerate(NEAR):
        sx, sy = box(thin_cut, d)
        send(part1.at[sx, sy], thin_in[other(d)], 4, i, d)
    sum_own2[...] = line_end(sum_own, line_in, 0, n_gx)
    line_start(sum_own2, line_in2, 1, n_gy, lambda d: (0, farthest(n_gy)[d - 1]))
    total = line_end(sum_own2, line_in2, 1, n_gy)

    def scalar(i):
        index = jnp.full((8, LANES), i, jnp.int32)
        return jnp.take_along_axis(
            jnp.broadcast_to(total, (8, LANES)), index, axis=1, mode="promise_in_bounds"
        )

    bz, zw, bu, wu, uv = (scalar(i) for i in range(5))
    step0 = bz / zw
    rz1 = bz - step0 * (bu + zw) + step0 * step0 * wu
    ratio = rz1 / bz
    mixed = zw - step0 * wu
    curve = zw - 2.0 * step0 * wu + step0 * step0 * uv + 2.0 * ratio * mixed + ratio * ratio * zw
    step1 = rz1 / curve
    first = (step0 + step1 + step1 * ratio)[0:3]
    second = (step1 * step0)[0:3]

    answer[...] = first * z - second * u
    for n in range(48):
        x, y, m = n // 12, n // 3 % 4, n % 3
        x_ref[m, x, y : y + 1, :] = answer[x, y, m : m + 1, :]
    e0_ref[0:4, 0:4] = part1[1:5, 1:5]
    for i, d in enumerate(NEAR):
        arrived(thin_in[i], 4, i)
        sx, sy = box(thin_place, d)
        e0_ref[sx, sy] = e0_ref[sx, sy] + thin_in[i][...] * kept(d)
    answer[...] = b - first * w + second * e0_ref[0:4, 0:4]
    for n in range(48):
        x, y, m = n // 12, n // 3 % 4, n % 3
        r_ref[m, x, y : y + 1, :] = answer[x, y, m : m + 1, :]
    close()


def solution(mesh):
    n_gx, n_gy = mesh.shape["gx"], mesh.shape["gy"]

    def vmem(*shape, dtype=F32):
        return pltpu.VMEM(shape, dtype)

    scratch = [vmem(*extent(first_cut, (-d[0], -d[1]), 4)) for d in NEAR]
    scratch += [
        vmem(len(CORNER), 3, LANES) if d[0] and d[1] else vmem(*extent(wide_cut, (-d[0], -d[1]), 3))
        for d in NEAR
    ]
    scratch += [vmem(*extent(thin_cut, (-d[0], -d[1]), 3)) for d in NEAR]
    scratch += [vmem(2, 2, 4, LANES) for _ in range(8)]
    scratch += [vmem(2, 2, 3, LANES) for _ in range(8)]
    scratch += [
        vmem(3, 4, 4, LANES), vmem(4, 4, LANES),
        vmem(8, LANES), vmem(8, LANES, dtype=jnp.int32), vmem(8, LANES, dtype=jnp.int32),
    ]
    scratch += [
        vmem(81, 8, LANES),
        vmem(4, 4, 4, LANES),
        vmem(10, 10, 3, LANES),
        vmem(10, 10, 3, LANES),
        vmem(10, 10, 1, LANES),
        vmem(10, 10, 3, LANES),
        vmem(10, 10, 3, LANES),
        vmem(2, 2, 4, LANES),
        vmem(2, 2, 3, LANES),
        vmem(6, 6, 3, LANES),
        vmem(6, 6, 3, LANES),
        vmem(1, LANES),
        vmem(1, LANES),
        vmem(9, 16, LANES),
        vmem(9, 16, LANES),
        vmem(9, 16, LANES),
        vmem(3, 16, LANES),
        vmem(6, 6, 3, LANES),
        vmem(6, 6, 3, LANES),
        vmem(3, 6, 6, 3, LANES),
        vmem(3 * ROWS * 8, LANES),
        vmem(LANES, 8 * LANES, dtype=BF16),
        vmem(ROWS, LANES),
        vmem(6, 6, 3, LANES),
        vmem(6, 6, 3, LANES),
        vmem(8, LANES),
        vmem(1, LANES),
        vmem(1, LANES),
        vmem(n_gx, 1, LANES),
        vmem(n_gy, 1, LANES),
        vmem(4, 4, 3, LANES),
        vmem(4, len(CORNER), 3, LANES),
        vmem(9, 1, LANES),
        vmem(8, 1, LANES),
        vmem(6, 6, 3, LANES),
        vmem(8, 8, 3, LANES),
        vmem(6, 6, 3, LANES),
        vmem(10, 16, LANES),
        vmem(10, 16, LANES),
        pltpu.SemaphoreType.DMA((6, 8)),
        pltpu.SemaphoreType.DMA((6, 8)),
        pltpu.SemaphoreType.DMA((2,)),
        pltpu.SemaphoreType.DMA((2,)),
        pltpu.SemaphoreType.DMA((2,)),
        pltpu.SemaphoreType.DMA((2,)),
        pltpu.SemaphoreType.DMA((6,)),
    ]

    def body(right, mass, gradients, *rest):
        by_tile = jnp.transpose(gradients[0, 0], (1, 2, 0, 3)).reshape(81, 8, LANES)
        args = (right, mass, by_tile) + rest
        call = pl.pallas_call(
            lambda *refs: kernel(n_gx, n_gy, *refs),
            out_shape=pltpu.VMEM((2, 3, 4, 4, LANES), F32),
            in_specs=[pl.BlockSpec(memory_space=pl.ANY)] * 6,
            out_specs=pl.BlockSpec(memory_space=pltpu.VMEM),
            scratch_shapes=scratch,
            compiler_params=pltpu.CompilerParams(collective_id=0, has_side_effects=True),
            name="cg",
        )
        both = call(*args)
        return both[0], both[1]

    field = P(None, "gx", "gy", None)
    block = P("gx", "gy", None, None)
    return jax.shard_map(
        body,
        mesh=mesh,
        in_specs=(field, P("gx", "gy", None), P("gx", "gy", None, None, None, None)) + (block,) * 3,
        out_specs=(field, field),
        check_vma=False,
    )
```
